32 devices in a mesh: fsdp: 4 (over z), seq: 8 (over y, x, core).
Axes of the slice: x: 2, y: 2, z: 4, core: 2. Of those that a mesh axis runs over, the one named last changes fastest.
Arguments:
- tokens: bfloat16 [4096, 2048], P(('fsdp', 'seq')), may hold values from -6 to 6
- cotangent: bfloat16 [4096, 2048], P(('fsdp', 'seq')), may hold values from -6 to 6
- gains: float32 [4, 2048], replicated, may hold values from 0.25 to 5
- w_qkv: bfloat16 [2048, 6144], P(('fsdp', 'seq')), may hold values from -0.088388348 to 0.088388348
- w_out: bfloat16 [2048, 2048], P(('fsdp', 'seq')), may hold values from -1 to 1
- w_router: bfloat16 [2048, 16], P(('fsdp', 'seq')), may hold values from -0.25 to 0.25
- w_gate: bfloat16 [16, 2048, 1024], P('seq', 'fsdp'), may hold values from -0.125 to 0.125
- w_up: bfloat16 [16, 2048, 1024], P('seq', 'fsdp'), may hold values from -0.125 to 0.125
- w_down: bfloat16 [16, 1024, 2048], P('seq', 'fsdp'), may hold values from -1.5 to 1.5
- routes: int32 [4096, 8], P(('fsdp', 'seq')), may hold values from 0 to 15, all different within a row; in each aligned block of 128 rows (0 to 127, 128 to 255, ...) at most 96 rows name the same one
Outputs:
- output: bfloat16 [4096, 2048], P(('fsdp', 'seq'))
- grad_tokens: float32 [4096, 2048], P(('fsdp', 'seq'))
- grad_gains: float32 [4, 2048], P(None, ('fsdp', 'seq'))
- grad_qkv: float32 [2048, 6144], P(('fsdp', 'seq'))
- grad_out: float32 [2048, 2048], P(('fsdp', 'seq'))
- grad_router: float32 [2048, 16], P(('fsdp', 'seq'))
- grad_gate: float32 [16, 2048, 1024], P('seq', 'fsdp')
- grad_up: float32 [16, 2048, 1024], P('seq', 'fsdp')
- grad_down: float32 [16, 1024, 2048], P('seq', 'fsdp')
The draws below stay inside these ranges and needn't reach their ends.
Inputs may be any that keep to these rules, and one draw needn't show every extreme that they name: `routes`: within a row the 8 experts differ. Among the rows of one device (aligned blocks of 128 rows) no expert is named more than 96 times, and in some such block one is named exactly 96 times.
All inputs are finite; a program needn't handle non-finite values.
Results may differ from the reference program's by a relative error of at most 0.02.
Values may be sent and summed in bfloat16 or wider, within the bound.
No kernel may reach another device: no remote copies, remote signals or barrier semaphores. Data moves between devices by JAX's collectives and lax.ppermute only.
A program may use at most 256 MiB of HBM per device.

```python
import math
from functools import partial
import jax
import jax.numpy as jnp
import numpy as np
from jax import lax

D = 2048
HEADS = 16
HEAD = 128
FF = 1024
TOP = 8
TOK_DEV = 128
QBLOCK = 512
EXPERTS = 16
CAP = 96
SEQLEN = 1024
TOKENS = 4096
N_FSDP = 4
N_SEQ = 8


def draw_gains(key, part):
    return jax.random.uniform(jax.random.fold_in(key, 1), (4, D), jnp.float32, 0.5, 1.5)


def draw_w_qkv(key, part):
    spread = D ** (-0.5)
    entries = jnp.clip(jax.random.normal(jax.random.fold_in(key, 3), (D, 3 * D), jnp.float32), -4.0, 4.0)
    return (entries * spread).astype(jnp.bfloat16)


def strengthened(array, own_key, source, target, shards_of, factor):
    owner, partner = [(jnp.arange(array.shape[axis_at]) // (array.shape[axis_at] // shards_of)).reshape([-1 if axis == axis_at else 1 for axis in range(array.ndim)]) for axis_at in (source, target)]
    chosen = jax.random.permutation(own_key, shards_of)[partner]
    strong = (owner == chosen) | (owner == (partner + shards_of // 2) % shards_of)
    return jnp.where(strong, factor * array, array)


def shard_levels(stream_key, dims, shards, low, top_value):
    gain, own = 1.0, jax.random.fold_in(stream_key, 6)
    for axis_at, parts in shards:
        draws = jnp.exp(jax.random.uniform(jax.random.fold_in(own, axis_at), (parts,), jnp.float32, low / len(shards), top_value / len(shards)))
        gain = gain * jnp.repeat(draws, dims[axis_at] // parts).reshape([-1 if axis == axis_at else 1 for axis in range(len(dims))])
    return gain


def routed_block(key, own, number, rows, number_of, top, reach, slope):
    sequence = jax.random.permutation(key, number_of)
    crowded, common = shares(number_of, rows * top, reach, slope, True), shares(number_of, rows * top, reach, slope, False)
    places = jnp.arange(number_of)

    def named(sizes, offset_by):
        used = int((sizes > 0).sum())
        fixed = max(1, used // 4)
        shifted = fixed + (places - fixed + offset_by * (used - fixed)) % max(1, number_of - fixed)
        return jnp.zeros((number_of,), jnp.int32).at[sequence[jnp.where(places < fixed, places, shifted)]].set(jnp.asarray(sizes, jnp.int32))

    sizes = jnp.where(number % 4 == 0, named(crowded, number // 4), named(common, number - number // 4 - 1))
    mixed = jax.random.permutation(jax.random.fold_in(own, 3), number_of)
    source_of, receiver = mixed[0:number_of // 2 * 2:2], mixed[1:number_of // 2 * 2:2]
    room = jnp.minimum(sizes[source_of] - 1, reach - sizes[receiver]) // 2
    room = jnp.where((source_of == sequence[0]) | (receiver == sequence[0]) | (sizes[receiver] == 0), 0, jnp.maximum(room, 0))
    shifted = jax.random.randint(jax.random.fold_in(own, 4), (number_of // 2,), 0, 1 << 20) % (room + 1)
    sizes = sizes.at[source_of].add(-shifted).at[receiver].add(shifted)
    members = jnp.searchsorted(jnp.cumsum(sizes), jnp.arange(rows * top), side="right").astype(jnp.int32)
    listing = members.reshape(top, rows).T
    listing = listing[jax.random.permutation(jax.random.fold_in(own, 1), rows)]
    offset_by = jax.random.randint(jax.random.fold_in(own, 2), (rows, 1), 0, top)
    return jnp.take_along_axis(listing, (jnp.arange(top)[None, :] + offset_by) % top, axis=1)


def shares(number_of, total, bound, lean, full):
    loads = [(1 << 20) // math.isqrt(standing ** lean) + 1 for standing in range(1, number_of + 1)]
    largest = bound if full else min(bound, max(-(-total // number_of), total * loads[0] // sum(loads)))
    least = 1 if total - largest >= number_of - 1 else 0
    counts, spare = [largest] + [least] * (number_of - 1), total - largest - least * (number_of - 1)
    while spare > 0:
        candidates = [i for i in range(1, number_of) if counts[i] < largest] or [i for i in range(1, number_of) if counts[i] < bound]
        pool, left = sum([loads[i] for i in candidates]), spare
        for i in candidates:
            addition = min(bound - counts[i], max(1, left * loads[i] // pool), spare)
            counts[i] = counts[i] + addition
            spare = spare - addition
    return np.array(counts)


def normal_values(stream_key, dims, scale, bound, shards=(), held_as=jnp.bfloat16):
    factor_of = shard_levels(stream_key, dims, shards, -0.22, 0.18) if shards else 1.0
    drawn = jax.random.normal(stream_key, dims, jnp.float32) * scale * factor_of
    return jnp.minimum(jnp.maximum(drawn, -bound), bound).astype(held_as)


def gaussian_with(own_key, extent, deviation, limit, cuts, heavy, held_as=jnp.bfloat16):
    values = deviation * jax.random.normal(own_key, extent, jnp.float32)
    if cuts:
        values = values * shard_levels(own_key, extent, cuts, -0.22, 0.18)
    return jnp.clip(strengthened(values, jax.random.fold_in(own_key, 3), *heavy), -limit, limit).astype(held_as)


def setup_inputs(seed: int = 0) -> dict:
    key_list = jax.random.split(jax.random.key(seed), 11)
    tokens = gaussian_with(key_list[0], (TOKENS, D), 1.0, 6.0, ((0, 32),), (0, 1, 32, 2.75))
    cotangent = normal_values(key_list[1], (TOKENS, D), 1.0, 6.0, ((0, 32),))
    gains = draw_gains(jax.random.fold_in(key_list[10], 71), 0)
    w_qkv = draw_w_qkv(jax.random.fold_in(key_list[10], 71), 0)
    w_out = normal_values(key_list[4], (D, D), (D // 64) ** -0.5, 1.0, ((0, 32),))
    w_router = normal_values(key_list[5], (D, EXPERTS), (D // 4) ** -0.5, 0.25, ((0, 32),))
    w_gate = normal_values(key_list[6], (EXPERTS, D, FF), D ** -0.5, 0.125, ((0, 8), (1, 4)))
    w_up = normal_values(key_list[7], (EXPERTS, D, FF), D ** -0.5, 0.125, ((0, 8), (1, 4)))
    w_down = normal_values(key_list[8], (EXPERTS, FF, D), (FF // 64) ** -0.5, 1.5, ((0, 8), (1, 4)))
    routes_keys = jax.random.split(jax.random.fold_in(key_list[9], 1), TOKENS // TOK_DEV)
    routes_turns = jax.random.permutation(jax.random.fold_in(key_list[9], 3), TOKENS // TOK_DEV)
    routes = jax.vmap(lambda own, number: routed_block(jax.random.fold_in(key_list[9], 2), own, number, TOK_DEV, EXPERTS, TOP, CAP, 2))(routes_keys, routes_turns).reshape((TOKENS, TOP))
    return {"tokens": tokens, "cotangent": cotangent, "gains": gains, "w_qkv": w_qkv, "w_out": w_out, "w_router": w_router, "w_gate": w_gate, "w_up": w_up, "w_down": w_down, "routes": routes}


epsilon = 1e-05
rotary_base = 10000.0

@jax.custom_vjp
def low(v):
    return lax.optimization_barrier(v.astype(jnp.bfloat16)).astype(jnp.float32)

@jax.custom_vjp
def low_back(v):
    return v

def low_keep(v):
    return (low(v), None)

def low_pass(kept, grad):
    return (grad,)

def back_keep(v):
    return (v, None)

def back_low(kept, grad):
    return (low(grad),)
low.defvjp(low_keep, low_pass)
low_back.defvjp(back_keep, back_low)

def rms_norm(values, gain_row):
    return values * lax.rsqrt(lax.optimization_barrier(jnp.mean(values * values, axis=-1, keepdims=True)) + epsilon) * gain_row

def rotary(values, position):
    half_width = values.shape[-1] // 2
    exponent_index = jnp.arange(half_width, dtype=jnp.float32) * (2.0 / values.shape[-1])
    angles = position[:, None] * (rotary_base ** (-exponent_index))[None, :]
    cosine = jnp.cos(angles)[:, None, :]
    sine_part = jnp.sin(angles)[:, None, :]
    first_half = values[..., :half_width]
    second = values[..., half_width:]
    return jnp.concatenate([first_half * cosine - second * sine_part, second * cosine + first_half * sine_part], axis=-1)

def slot_table(route_rows, expert_count, capacity):
    route_flat = route_rows.reshape(-1)
    pick_count = route_flat.shape[0]
    onehot = (route_flat[:, None] == jnp.arange(expert_count, dtype=jnp.int32)[None, :]).astype(jnp.int32)
    before = lax.optimization_barrier(jnp.sum((jnp.cumsum(onehot, axis=0) - onehot) * onehot, axis=1))
    slot_index = route_flat * capacity + before
    matches = slot_index[None, :] == jnp.arange(expert_count * capacity, dtype=jnp.int32)[:, None]
    token_of = jnp.arange(pick_count, dtype=jnp.int32) // route_rows.shape[1]
    owner_row = lax.optimization_barrier(jnp.sum(jnp.where(matches, token_of[None, :], 0), axis=1)).astype(jnp.int32)
    filled = jnp.any(matches, axis=1)
    return (slot_index, owner_row, filled, matches)

def attend(query_low, key_low, value_low):
    score_scale = HEAD ** (-0.5)
    key_pos = jnp.arange(SEQLEN, dtype=jnp.int32)

    def one_block(first_row):
        query_block = lax.dynamic_slice_in_dim(query_low, first_row, QBLOCK, 0)
        scores = jnp.einsum('qhd,khd->hqk', query_block, key_low, precision=lax.Precision.HIGHEST) * score_scale
        scores = low_back(scores)
        query_pos = first_row + jnp.arange(QBLOCK, dtype=jnp.int32)
        scores = jnp.where((key_pos[None, :] <= query_pos[:, None])[None], scores, -jnp.inf)
        row_peak = lax.optimization_barrier(jnp.max(scores, axis=-1, keepdims=True))
        exponent = jnp.exp(scores - row_peak)
        weights = low(exponent / lax.optimization_barrier(jnp.sum(exponent, axis=-1, keepdims=True)))
        return jnp.einsum('hqk,khd->qhd', weights, value_low, precision=lax.Precision.HIGHEST)
    outputs = lax.map(jax.checkpoint(one_block), jnp.arange(SEQLEN // QBLOCK, dtype=jnp.int32) * QBLOCK)
    return outputs.reshape(SEQLEN, HEADS, HEAD)

def mixture(normed, route_rows, route_prob, weight_gate, weight_up, weight_down):
    slot_index, owner_row, filled, matches = jax.vmap(partial(slot_table, expert_count=EXPERTS, capacity=CAP))(route_rows)
    gathered = jax.vmap(lambda rows_in, pick_rows: jnp.take(rows_in, pick_rows, axis=0))(normed, owner_row)
    buffers = low_back(jnp.where(filled[..., None], gathered, jnp.zeros((), jnp.float32)))
    grouped = buffers.reshape(N_SEQ, EXPERTS, CAP, D).transpose(1, 0, 2, 3).reshape(EXPERTS, N_SEQ * CAP, D)
    gate_value = low_back(jnp.einsum('erd,edf->erf', grouped, weight_gate, precision=lax.Precision.HIGHEST))
    up_value = low_back(jnp.einsum('erd,edf->erf', grouped, weight_up, precision=lax.Precision.HIGHEST))
    activated = low(jax.nn.silu(gate_value) * up_value)
    expert_out = low_back(low(jnp.einsum('erf,efd->erd', activated, weight_down, precision=lax.Precision.HIGHEST)))
    returned = expert_out.reshape(EXPERTS, N_SEQ, CAP, D).transpose(1, 0, 2, 3).reshape(N_SEQ, EXPERTS * CAP, D)
    picked = jax.vmap(lambda rows_in, pick_rows: jnp.take(rows_in, pick_rows, axis=0))(returned, slot_index)
    picked = picked.reshape(N_SEQ, TOK_DEV, TOP, D)
    return lax.optimization_barrier(jnp.sum(route_prob[..., None] * picked, axis=2))

def block_layer(inputs, route_rows, gain_rows, weight_qkv, weight_out, weight_router, weight_gate, weight_up, weight_down):
    normed_attn = low(rms_norm(inputs, gain_rows[0]))
    projected = low_back(jnp.dot(normed_attn, weight_qkv, precision=lax.Precision.HIGHEST))
    position = jnp.arange(SEQLEN, dtype=jnp.int32).astype(jnp.float32)
    query_rot = rotary(rms_norm(projected[:, :D], gain_rows[1]).reshape(SEQLEN, HEADS, HEAD), position)
    key_rot = rotary(rms_norm(projected[:, D:2 * D], gain_rows[2]).reshape(SEQLEN, HEADS, HEAD), position)
    query_low = low_back(low(query_rot))
    key_low = low_back(low(key_rot))
    value_low = low_back(low(projected[:, 2 * D:].reshape(SEQLEN, HEADS, HEAD)))
    attended = attend(query_low, key_low, value_low)
    mixed_heads = low_back(low(attended)).reshape(SEQLEN, D)
    residual = inputs + low_back(jnp.dot(mixed_heads, weight_out, precision=lax.Precision.HIGHEST))
    normed_ffn = low(rms_norm(residual, gain_rows[3]))
    logits = low_back(jnp.dot(normed_ffn, weight_router, precision=lax.Precision.HIGHEST))
    router_probs = jax.nn.softmax(logits, axis=-1)
    route_prob = jnp.take_along_axis(router_probs, route_rows.reshape(SEQLEN, TOP), axis=1)
    moe_out = mixture(normed_ffn.reshape(N_SEQ, TOK_DEV, D), route_rows, route_prob.reshape(N_SEQ, TOK_DEV, TOP), weight_gate, weight_up, weight_down)
    return residual + moe_out.reshape(SEQLEN, D)

def forward(inputs, gain_rows, weight_qkv, weight_out, weight_router, weight_gate, weight_up, weight_down, routes):
    sequences = inputs.reshape(N_FSDP, SEQLEN, D)
    route_seqs = routes.reshape(N_FSDP, N_SEQ, TOK_DEV, TOP)

    def one_sequence(carried, sequence_item):
        return (carried, block_layer(sequence_item[0], sequence_item[1], gain_rows, weight_qkv, weight_out, weight_router, weight_gate, weight_up, weight_down))
    carried_out, results = lax.scan(one_sequence, jnp.zeros((), jnp.float32), (sequences, route_seqs))
    return results.reshape(TOKENS, D)

def reference(tokens, cotangent, gains, w_qkv, w_out, w_router, w_gate, w_up, w_down, routes):

    def with_routes(inputs, gain_rows, weight_qkv, weight_out, weight_router, weight_gate, weight_up, weight_down):
        return forward(inputs, gain_rows, weight_qkv, weight_out, weight_router, weight_gate, weight_up, weight_down, routes)
    output, pullback = jax.vjp(with_routes, tokens.astype(jnp.float32), gains, w_qkv.astype(jnp.float32), w_out.astype(jnp.float32), w_router.astype(jnp.float32), w_gate.astype(jnp.float32), w_up.astype(jnp.float32), w_down.astype(jnp.float32))
    gradients = pullback(cotangent.astype(jnp.float32))
    return (output.astype(jnp.bfloat16), gradients[0], gradients[1], gradients[2], gradients[3], gradients[4], gradients[5], gradients[6], gradients[7])
```

```python
import functools

import jax
import jax.numpy as jnp
from jax import lax
from jax.experimental import pallas as pl
from jax.experimental.pallas import tpu as pltpu
from jax.sharding import Mesh, PartitionSpec as P


HEAD = 128
LANES = 128

BF16 = jnp.bfloat16
F32 = jnp.float32

epsilon = 1e-05
rotary_base = 10000.0

SEQ = ("q", "c")


def mm(a, b, ca, cb):
    return lax.dot_general(a, b, (((ca,), (cb,)), ((), ())), preferred_element_type=F32)


def swap(value, axis, count, k):
    return lax.ppermute(value, axis, [(i, i ^ k) for i in range(count)])


def after(value, *others):
    return lax.optimization_barrier((value, *others))[0]


def vmem_params(count):
    return pltpu.CompilerParams(
        dimension_semantics=("arbitrary",) * count, vmem_limit_bytes=60 * 1024 * 1024
    )


def held(shape, index_map):
    return pl.BlockSpec(shape, index_map, pipeline_mode=pl.Buffered(1))


def cost(flops, nbytes):
    return pl.CostEstimate(flops=int(flops), bytes_accessed=int(nbytes), transcendentals=0)


def pack_kernel(where, gate_ref, up_ref, *out_refs):
    planes = len(out_refs)
    size = gate_ref.shape[2] // planes
    for k in range(planes):
        columns = pl.ds(pl.multiple_of((where[0] ^ k) * size, 128), size)
        out_refs[k][:, :size] = gate_ref[0, :, columns]
        out_refs[k][:, size:] = up_ref[0, :, columns]


def pack_experts(where, w_gate, w_up, planes):
    experts, slab, full = w_gate.shape
    size = full // planes
    spec = pl.BlockSpec((1, slab, full), lambda e, s: (e, 0, 0))
    out = pl.BlockSpec((slab, 2 * size), lambda e, s: (0, e))
    return pl.pallas_call(
        pack_kernel,
        grid_spec=pltpu.PrefetchScalarGridSpec(
            num_scalar_prefetch=1, grid=(experts,), in_specs=[spec, spec], out_specs=[out] * planes
        ),
        out_shape=[jax.ShapeDtypeStruct((slab, 2 * experts * size), BF16)] * planes,
        compiler_params=vmem_params(1),
        name="pack_experts",
    )(where, w_gate, w_up)


def place_kernel(where, *refs):
    out_ref = refs[-1]
    for k, piece in enumerate(refs[:-1]):
        size = piece.shape[0]
        out_ref[pl.ds(pl.multiple_of((where[0] ^ k) * size, 128), size), :] = piece[...]


def place_rows(where, pieces):
    rows, columns = pieces[0].shape
    full = rows * len(pieces)
    half = columns // 2
    return pl.pallas_call(
        place_kernel,
        grid_spec=pltpu.PrefetchScalarGridSpec(
            num_scalar_prefetch=1,
            grid=(2,),
            in_specs=[pl.BlockSpec((rows, half), lambda i, s: (0, i))] * len(pieces),
            out_specs=pl.BlockSpec((full, half), lambda i, s: (0, i)),
        ),
        out_shape=jax.ShapeDtypeStruct((full, columns), BF16),
        compiler_params=vmem_params(1),
        name="place_rows",
    )(where, *pieces)


def unpack_kernel(where, *refs):
    gate_ref, up_ref = refs[-2:]
    size = refs[0].shape[1] // 2
    for k, piece in enumerate(refs[:-2]):
        columns = pl.ds(pl.multiple_of((where[0] ^ k) * size, 128), size)
        gate_ref[0, :, columns] = piece[:, :size].astype(F32)
        up_ref[0, :, columns] = piece[:, size:].astype(F32)


def unpack_experts(where, pieces, experts):
    slab, columns = pieces[0].shape
    size = columns // (2 * experts)
    full = size * len(pieces)
    spec = pl.BlockSpec((slab, 2 * size), lambda e, s: (0, e))
    out = pl.BlockSpec((1, slab, full), lambda e, s: (e, 0, 0))
    shape = jax.ShapeDtypeStruct((experts, slab, full), F32)
    return pl.pallas_call(
        unpack_kernel,
        grid_spec=pltpu.PrefetchScalarGridSpec(
            num_scalar_prefetch=1,
            grid=(experts,),
            in_specs=[spec] * len(pieces),
            out_specs=[out, out],
        ),
        out_shape=[shape, shape],
        compiler_params=vmem_params(1),
        name="unpack_experts",
    )(where, *pieces)


def moe_kernel(count, experts, own_experts, aliased, where, *refs):
    x_refs, y_refs = refs[:count], refs[count : 2 * count]
    router_ref = refs[2 * count]
    gu_refs, down_refs = refs[2 * count + 1 : 2 * count + 3], refs[2 * count + 3 : 2 * count + 5]
    refs = refs[2 * count + 5 + (count if aliased else 0) :]
    dx_refs, out_refs = refs[:count], refs[count : 2 * count]
    act_ref, grad_ref = refs[2 * count : 2 * count + 2]
    xs, ys, gu_all, down_all, prob_sum, sems = refs[2 * count + 2 :]
    rows, width = x_refs[0].shape
    steps, size = down_all.shape[:2]

    for e in range(steps):
        side, i = divmod(e, own_experts)
        cols = slice(i * 2 * size, (i + 1) * 2 * size)
        lines = slice(i * size, (i + 1) * size)
        pltpu.make_async_copy(gu_refs[side].at[:, cols], gu_all.at[e], sems.at[0, e]).start()
        pltpu.make_async_copy(down_refs[side].at[lines, :], down_all.at[e], sems.at[1, e]).start()
    for i in range(count):
        here = slice(i * rows, (i + 1) * rows)
        xs[here, :] = x_refs[i][...]
        ys[here, :] = y_refs[i][:, :width]
    logits = mm(xs[...], router_ref[...], 1, 0)
    lane = lax.broadcasted_iota(jnp.int32, logits.shape, 1)
    logits = jnp.where(lane < experts, logits, -jnp.inf)
    spread = jnp.exp(logits - jnp.max(logits, axis=1, keepdims=True))
    probs = spread / jnp.sum(spread, axis=1, keepdims=True)
    weight = probs * jnp.concatenate([y[:, width:].astype(F32) for y in y_refs], axis=0)
    prob_sum[...] = jnp.zeros_like(prob_sum)

    def one_expert(e, carry):
        pltpu.make_async_copy(gu_all.at[e], gu_all.at[e], sems.at[0, e]).wait()
        pltpu.make_async_copy(down_all.at[e], down_all.at[e], sems.at[1, e]).wait()
        which = jnp.where(
            e < own_experts,
            where[1] * own_experts + e,
            (where[1] ^ 1) * own_experts + e - own_experts,
        )
        prob = jnp.sum(jnp.where(lane == which, weight, 0.0), axis=1, keepdims=True)
        both = mm(xs[...], gu_all[e], 1, 0)
        gate, up = both[:, :size], both[:, size:]
        sig = 1.0 / (1.0 + jnp.exp(-gate))
        back = mm(ys[...], down_all[e], 1, 1)
        silu = gate * sig
        act = silu * up
        prob_sum[...] += jnp.where(lane == which, jnp.sum(act * back, axis=1, keepdims=True), 0.0)
        back = back * prob
        act_ref[:, pl.ds(pl.multiple_of(e * size, size), size)] = (act * prob).astype(BF16)
        grad_ref[:, pl.ds(pl.multiple_of(2 * e * size, size), size)] = (
            back * up * sig * (1.0 + gate * (1.0 - sig))
        ).astype(BF16)
        grad_ref[:, pl.ds(pl.multiple_of((2 * e + 1) * size, size), size)] = (back * silu).astype(
            BF16
        )
        return carry

    lax.fori_loop(0, steps, one_expert, 0)
    tile = min(512, width)

    def one_tile(n, carry):
        cols = pl.ds(pl.multiple_of(n * tile, tile), tile)
        dx = out = None
        for e in range(steps):
            term = mm(grad_ref[:, 2 * e * size : 2 * (e + 1) * size], gu_all[e, cols, :], 1, 1)
            dx = term if dx is None else dx + term
            term = mm(act_ref[:, e * size : (e + 1) * size], down_all[e, :, cols], 1, 0)
            out = term if out is None else out + term
        for i in range(count):
            here = slice(i * rows, (i + 1) * rows)
            dx_refs[i][:, cols] = dx[here].astype(BF16)
            out_refs[i][:, cols] = out[here].astype(BF16)
        return carry

    lax.fori_loop(0, width // tile, one_tile, 0)
    for i in range(count):
        dx_refs[i][:, width:] = prob_sum[i * rows : (i + 1) * rows].astype(BF16)


def moe_rows(where, group, groups, xs, ys, router, gus, downs, outs, experts, own_experts):
    count = len(xs)
    rows, width = xs[0].shape
    size = downs[0].shape[0] // own_experts
    total = count * rows
    steps = 2 * own_experts
    lanes = router.shape[1]
    aliased = outs is not None

    def fixed(block):
        return lambda i, s: (block, 0)

    anywhere = pl.BlockSpec(memory_space=pl.ANY)
    in_specs = (
        [held((rows, width), fixed(0)) for _ in xs]
        + [held((rows, y.shape[1]), fixed(i)) for y, i in ys]
        + [held(router.shape, fixed(0))]
        + [anywhere] * 4
        + ([anywhere] * count if aliased else [])
    )
    out_specs = (
        [held((rows, width + lanes), fixed(0))] * count
        + [held((rows, width), fixed(group))] * count
        + [held((total, steps * size), fixed(0)), held((total, 2 * steps * size), fixed(0))]
    )
    first = 1 + 2 * count + 5
    return pl.pallas_call(
        functools.partial(moe_kernel, count, experts, own_experts, aliased),
        grid_spec=pltpu.PrefetchScalarGridSpec(
            num_scalar_prefetch=1,
            grid=(1,),
            in_specs=in_specs,
            out_specs=out_specs,
            scratch_shapes=[
                pltpu.VMEM((total, width), BF16),
                pltpu.VMEM((total, width), BF16),
                pltpu.VMEM((steps, width, 2 * size), BF16),
                pltpu.VMEM((steps, size, width), BF16),
                pltpu.VMEM((total, lanes), F32),
                pltpu.SemaphoreType.DMA((2, steps)),
            ],
        ),
        out_shape=[jax.ShapeDtypeStruct((rows, width + lanes), BF16)] * count
        + [jax.ShapeDtypeStruct((groups * rows, width), BF16)] * count
        + [
            jax.ShapeDtypeStruct((total, steps * size), BF16),
            jax.ShapeDtypeStruct((total, 2 * steps * size), BF16),
        ],
        input_output_aliases={first + i: count + i for i in range(count)} if aliased else {},
        compiler_params=vmem_params(1),
        cost_estimate=cost(
            12 * total * width * size * steps, 8 * total * width + 6 * width * size * steps
        ),
        name="moe_rows",
    )(where, *xs, *[y for y, _ in ys], router, *gus, *downs, *(outs or []))


def norm_ffn_kernel(token_ref, own_ref, *refs):
    gain_ref, res_ref, low_ref = refs[-3:]
    total = token_ref[...].astype(F32) + own_ref[...]
    for ref in refs[:-3]:
        total = total + ref[...].astype(F32)
    res_ref[...] = total
    scale = lax.rsqrt(jnp.mean(total * total, axis=1, keepdims=True) + epsilon)
    low_ref[...] = (total * scale * gain_ref[...]).astype(BF16)


def norm_ffn(tokens, own, parts, gain):
    return pl.pallas_call(
        norm_ffn_kernel,
        out_shape=[
            jax.ShapeDtypeStruct(tokens.shape, F32),
            jax.ShapeDtypeStruct(tokens.shape, BF16),
        ],
        compiler_params=vmem_params(0),
        cost_estimate=cost(10 * tokens.size, 16 * tokens.size),
        name="norm_ffn",
    )(tokens, own, *parts, gain)


def norm_back_kernel(experts, low_ref, res_ref, router_ref, wide_ref, gain_ref, *refs):
    grad_ref, grad_low_ref, logit_ref, gain_out = refs[-4:]
    width = res_ref.shape[1]
    total = refs[0][...].astype(F32)
    for ref in refs[1:-4]:
        total = total + ref[...].astype(F32)
    upstream = wide_ref[:, :width].astype(F32)
    mask = wide_ref[:, width:].astype(F32)
    logits = mm(low_ref[...], router_ref[...], 1, 0)
    lane = lax.broadcasted_iota(jnp.int32, logits.shape, 1)
    logits = jnp.where(lane < experts, logits, -jnp.inf)
    spread = jnp.exp(logits - jnp.max(logits, axis=1, keepdims=True))
    probs = spread / jnp.sum(spread, axis=1, keepdims=True)
    prob_full = total[:, width:] * mask
    logit = (
        probs * (prob_full - jnp.sum(probs * prob_full, axis=1, keepdims=True))
    ).astype(BF16)
    logit_ref[...] = logit
    dn = total[:, :width] + mm(logit, router_ref[...], 1, 1)
    residual = res_ref[...]
    scale = lax.rsqrt(jnp.mean(residual * residual, axis=1, keepdims=True) + epsilon)
    scaled = dn * gain_ref[...]
    grad = upstream + (
        scaled * scale - residual * (scale**3 * jnp.mean(residual * scaled, axis=1, keepdims=True))
    )
    grad_ref[...] = grad
    grad_low_ref[...] = grad.astype(BF16)
    gain_out[...] = jnp.sum(dn * residual * scale, axis=0, keepdims=True)


def norm_back(low, residual, router, wide, gain, parts, experts):
    count, width = residual.shape
    return pl.pallas_call(
        functools.partial(norm_back_kernel, experts),
        out_shape=[
            jax.ShapeDtypeStruct((count, width), F32),
            jax.ShapeDtypeStruct((count, width), BF16),
            jax.ShapeDtypeStruct((count, router.shape[1]), BF16),
            jax.ShapeDtypeStruct((1, width), F32),
        ],
        compiler_params=vmem_params(0),
        cost_estimate=cost(20 * low.size, 30 * low.size),
        name="norm_back",
    )(low, residual, router, wide, gain, *parts)


def merge_kernel(planes, where, own_ref, other_ref, *out_refs):
    total = own_ref[...].astype(F32) + other_ref[...].astype(F32)
    k = pl.program_id(0)
    for i in range(planes):

        @pl.when(k == i)
        def _(i=i):
            out_refs[i][...] = total.astype(BF16)


def merge_parts(where, own, other, planes):
    slab, columns = own.shape[0] // planes, own.shape[1]
    spec = pl.BlockSpec((slab, columns), lambda k, s: (s[0] ^ k, 0))
    return pl.pallas_call(
        functools.partial(merge_kernel, planes),
        grid_spec=pltpu.PrefetchScalarGridSpec(
            num_scalar_prefetch=1,
            grid=(planes,),
            in_specs=[spec, spec],
            out_specs=[pl.BlockSpec((slab, columns), lambda k, s: (0, 0))] * planes,
        ),
        out_shape=[jax.ShapeDtypeStruct((slab, columns), BF16)] * planes,
        compiler_params=vmem_params(1),
        cost_estimate=cost(own.size, 6 * own.size),
        name="merge_parts",
    )(where, own, other)


def grad_in_kernel(groups, count, where, *refs):
    x_refs = refs[: groups * count]
    g_refs = refs[groups * count : groups * count + groups]
    own_ref, other_ref, xs = refs[groups * count + groups :]
    rows = x_refs[0].shape[0]
    half = own_ref.shape[1]
    for i, x in enumerate(x_refs):
        xs[i * rows : (i + 1) * rows, :] = x[...]
    step = count * rows
    for out, start in ((own_ref, 0), (other_ref, half)):
        total = None
        for g in range(groups):
            term = mm(
                xs[g * step : (g + 1) * step, :], g_refs[g][:, start : start + half], 0, 0
            )
            total = term if total is None else total + term
        out[...] = total.astype(BF16)


def grad_in(where, xs, grads, tile=256):
    groups, count = len(grads), len(xs) // len(grads)
    rows, width = xs[0].shape
    columns = grads[0].shape[1]
    shape = jax.ShapeDtypeStruct((width, columns // 2), BF16)
    return pl.pallas_call(
        functools.partial(grad_in_kernel, groups, count),
        grid_spec=pltpu.PrefetchScalarGridSpec(
            num_scalar_prefetch=1,
            grid=(width // tile,),
            in_specs=[pl.BlockSpec((rows, tile), lambda i, s: (0, i))] * len(xs)
            + [held(g.shape, lambda i, s: (0, 0)) for g in grads],
            out_specs=[pl.BlockSpec((tile, columns // 2), lambda i, s: (i, 0))] * 2,
            scratch_shapes=[pltpu.VMEM((rows * len(xs), tile), BF16)],
        ),
        out_shape=[shape, shape],
        compiler_params=vmem_params(1),
        cost_estimate=cost(
            2 * rows * len(xs) * width * columns, 2 * rows * len(xs) * (width + columns)
        ),
        name="grad_in",
    )(where, *xs, *grads)


def grad_down_kernel(places, own_steps, where, *refs):
    y_refs = refs[: len(places)]
    groups = len(refs) - len(places) - 3
    a_refs = refs[len(places) : len(places) + groups]
    own_ref, other_ref, ys = refs[len(places) + groups :]
    e = pl.program_id(1)

    @pl.when(e == 0)
    def _():
        for ref, there in zip(y_refs, places):
            size = ref.shape[0] // len(there)
            for i, place in enumerate(there):
                ys[place * size : (place + 1) * size, :] = ref[i * size : (i + 1) * size, :]

    step = a_refs[0].shape[0]
    total = None
    for g in range(groups):
        term = mm(a_refs[g][...], ys[g * step : (g + 1) * step, :], 0, 0)
        total = term if total is None else total + term

    @pl.when(e < own_steps)
    def _():
        own_ref[...] = total

    @pl.when(e >= own_steps)
    def _():
        other_ref[...] = total.astype(BF16)


def grad_down_rows(where, ys, places, acts, width, own_experts):
    size = acts[0].shape[1] // (2 * own_experts)
    last = own_experts - 1
    total = acts[0].shape[0] * len(acts)
    tile = width
    while total * tile > 1 << 21:
        tile //= 2
    return pl.pallas_call(
        functools.partial(grad_down_kernel, places, own_experts),
        grid_spec=pltpu.PrefetchScalarGridSpec(
            num_scalar_prefetch=1,
            grid=(width // tile, 2 * own_experts),
            in_specs=[pl.BlockSpec((y.shape[0], tile), lambda j, e, s: (0, j)) for y in ys]
            + [pl.BlockSpec((a.shape[0], size), lambda j, e, s: (0, e)) for a in acts],
            out_specs=[
                pl.BlockSpec((size, tile), lambda j, e, s: (jnp.minimum(e, last), j)),
                pl.BlockSpec((size, tile), lambda j, e, s: (jnp.maximum(e - own_experts, 0), j)),
            ],
            scratch_shapes=[pltpu.VMEM((total, tile), BF16)],
        ),
        out_shape=[
            jax.ShapeDtypeStruct((own_experts * size, width), F32),
            jax.ShapeDtypeStruct((own_experts * size, width), BF16),
        ],
        compiler_params=vmem_params(2),
        cost_estimate=cost(
            4 * total * width * size * own_experts, 2 * total * (width + 2 * size * own_experts)
        ),
        name="grad_down_rows",
    )(where, *ys, *acts)


def block_rows(seq, block, seqs, size):
    k = seq ^ block
    return pl.ds(pl.multiple_of(((k & 1) * (seqs // 2) + (k >> 1)) * size, size), size)


def turned(values, cosine, sine):
    return values * cosine + pltpu.roll(values, values.shape[1] // 2, 1) * sine


def attend_kernel(seqs, tile, where, q_ref, k_ref, v_ref, scale_ref, gain_ref, cos_ref, sin_ref, att_ref, ql, kl, vl, lse_ref):
    length, head = q_ref.shape
    size = length // seqs
    for b in range(seqs):
        rows = block_rows(where[1], b, seqs, size)
        here = slice(b * size, (b + 1) * size)
        cosine, sine = cos_ref[here, :], sin_ref[here, :]
        scales = scale_ref[here, :]
        ql[here, :] = turned(
            q_ref[rows, :] * scales[:, 0:1] * gain_ref[0:1, :], cosine, sine
        ).astype(BF16)
        kl[here, :] = turned(
            k_ref[rows, :] * scales[:, 1:2] * gain_ref[1:2, :], cosine, sine
        ).astype(BF16)
        vl[here, :] = v_ref[rows, :].astype(BF16)
    diagonal = lax.broadcasted_iota(jnp.int32, (tile, tile), 0) >= lax.broadcasted_iota(
        jnp.int32, (tile, tile), 1
    )
    for t in range(length // tile):
        here = slice(t * tile, (t + 1) * tile)
        limit = (t + 1) * tile
        scores = mm(ql[here, :], kl[:limit, :], 1, 1) * (head ** (-0.5))
        edge = jnp.where(diagonal, scores[:, t * tile :], -jnp.inf)
        scores = jnp.concatenate([scores[:, : t * tile], edge], axis=1) if t else edge
        peak = jnp.max(scores, axis=1, keepdims=True)
        spread = jnp.exp(scores - peak)
        total = jnp.sum(spread, axis=1, keepdims=True)
        weights = (spread * (1.0 / total)).astype(BF16)
        out = mm(weights, vl[:limit, :], 1, 0).astype(BF16)
        lse_ref[here, :] = jnp.broadcast_to(peak + jnp.log(total), (tile, head))
        for b in range(tile // size):
            rows = block_rows(where[1], t * (tile // size) + b, seqs, size)
            att_ref[rows, :] = out[b * size : (b + 1) * size]


def attend(where, projected, scales, gain_rows, cosine, sine, seqs, heads, tile=256):
    length = projected.shape[0]
    head = projected.shape[1] // (3 * heads)
    part = heads * head

    def column(offset):
        return pl.BlockSpec((length, head), lambda h, s: (0, offset + h))

    full = pl.BlockSpec((length, head), lambda h, s: (0, 0))
    low = jax.ShapeDtypeStruct((length, part), BF16)
    return pl.pallas_call(
        functools.partial(attend_kernel, seqs, tile),
        grid_spec=pltpu.PrefetchScalarGridSpec(
            num_scalar_prefetch=1,
            grid=(heads,),
            in_specs=[
                column(0),
                column(heads),
                column(2 * heads),
                pl.BlockSpec(scales.shape, lambda h, s: (0, 0)),
                pl.BlockSpec((2, head), lambda h, s: (0, h)),
                full,
                full,
            ],
            out_specs=[column(0)] * 5,
        ),
        out_shape=[low, low, low, low, jax.ShapeDtypeStruct((length, part), F32)],
        compiler_params=vmem_params(1),
        cost_estimate=cost(4 * length * length * part, 20 * length * part),
        name="attend",
    )(where, projected, projected, projected, scales, gain_rows, cosine, sine)


def attend_back_kernel(seqs, tile, where, q_ref, k_ref, v_ref, lse_ref, grad_ref, cos_ref, sin_ref, dq_ref, dk_ref, dv_ref, go, dk, dv):
    length, head = q_ref.shape
    size = length // seqs
    scale = head ** (-0.5)
    for b in range(seqs):
        go[b * size : (b + 1) * size, :] = grad_ref[block_rows(where[1], b, seqs, size), :]
    dk[...] = jnp.zeros_like(dk)
    dv[...] = jnp.zeros_like(dv)
    diagonal = lax.broadcasted_iota(jnp.int32, (tile, tile), 0) >= lax.broadcasted_iota(
        jnp.int32, (tile, tile), 1
    )
    for t in range(length // tile):
        here = slice(t * tile, (t + 1) * tile)
        limit = (t + 1) * tile
        scores = mm(q_ref[here, :], k_ref[:limit, :], 1, 1) * scale
        edge = jnp.where(diagonal, scores[:, t * tile :], -jnp.inf)
        scores = jnp.concatenate([scores[:, : t * tile], edge], axis=1) if t else edge
        probs = jnp.exp(scores - lse_ref[here, 0:1])
        dprobs = mm(go[here, :], v_ref[:limit, :], 1, 1)
        terms = probs * dprobs
        dscores = (terms - probs * jnp.sum(terms, axis=1, keepdims=True)).astype(BF16)
        dq = (mm(dscores, k_ref[:limit, :], 1, 0) * scale).astype(BF16).astype(F32)
        dq = turned(dq, cos_ref[here, :], -sin_ref[here, :])
        for b in range(tile // size):
            rows = block_rows(where[1], t * (tile // size) + b, seqs, size)
            dq_ref[rows, :] = dq[b * size : (b + 1) * size]
        dk[:limit, :] += mm(dscores, q_ref[here, :], 0, 0)
        dv[:limit, :] += mm(probs.astype(BF16), go[here, :], 0, 0)
    for b in range(seqs):
        here = slice(b * size, (b + 1) * size)
        rows = block_rows(where[1], b, seqs, size)
        back = (dk[here, :] * scale).astype(BF16).astype(F32)
        dk_ref[rows, :] = turned(back, cos_ref[here, :], -sin_ref[here, :])
        dv_ref[rows, :] = dv[here, :].astype(BF16)


def attend_back(where, ql, kl, vl, lse, grads, cosine, sine, seqs, heads, tile=256):
    length, part = ql.shape
    head = part // heads
    column = pl.BlockSpec((length, head), lambda h, s: (0, h))
    full = pl.BlockSpec((length, head), lambda h, s: (0, 0))
    wide = jax.ShapeDtypeStruct((length, part), F32)
    return pl.pallas_call(
        functools.partial(attend_back_kernel, seqs, tile),
        grid_spec=pltpu.PrefetchScalarGridSpec(
            num_scalar_prefetch=1,
            grid=(heads,),
            in_specs=[column] * 5 + [full, full],
            out_specs=[column] * 3,
            scratch_shapes=[
                pltpu.VMEM((length, head), BF16),
                pltpu.VMEM((length, head), F32),
                pltpu.VMEM((length, head), F32),
            ],
        ),
        out_shape=[wide, wide, jax.ShapeDtypeStruct((length, part), BF16)],
        compiler_params=vmem_params(1),
        cost_estimate=cost(10 * length * length * part, 24 * length * part),
        name="attend_back",
    )(where, ql, kl, vl, lse, grads, cosine, sine)


def seq_gather(block, chips):
    near = [block] + [swap(block, "q", chips, k) for k in range(1, chips)]
    near = jnp.concatenate(near, axis=0)
    return near, swap(near, "c", 2, 1)


def seq_parts(own, other, chips):
    total = own + swap(other, "c", 2, 1).astype(F32)
    rows = total.shape[0] // chips
    low = total[rows:].astype(BF16)
    parts = [swap(low[(k - 1) * rows : k * rows], "q", chips, k) for k in range(1, chips)]
    return total[:rows], parts


def by_bits(values, index, axis):
    size = values.shape[axis]
    bit = 1
    while bit < size:
        turned_over = jnp.take(values, jnp.array([i ^ bit for i in range(size)]), axis=axis)
        values = jnp.where((index & bit) > 0, turned_over, values)
        bit *= 2
    return values


def to_position(values, seq, chips):
    n = values.shape[0]
    values = values.reshape(n, 2, chips, -1)
    values = by_bits(by_bits(values, seq & 1, 1), seq >> 1, 2)
    return values.swapaxes(1, 2).reshape(n, -1)


def from_position(values, seq, chips):
    n = values.shape[0]
    values = values.reshape(n, chips, 2, -1).swapaxes(1, 2)
    return by_bits(by_bits(values, seq & 1, 1), seq >> 1, 2).reshape(n, -1)


def small_sum(pair, seq, chips, rider=None):
    flat = to_position(pair, seq, chips).reshape(-1, LANES)
    count = flat.shape[0]
    if rider is not None:
        flat = jnp.concatenate([flat, rider.reshape(-1, LANES)], axis=0)
    every = lax.all_gather(flat, SEQ, axis=0)
    total = jnp.sum(every[:, :count], axis=0).reshape(pair.shape)
    return total if rider is None else (total, every[:, count:])


def shards(tokens, cotangent, gains, w_qkv, w_out, w_router, w_gate, w_up, w_down, routes):
    planes = lax.axis_size("f")
    chips = lax.axis_size("q")
    seqs = 2 * chips
    plane = lax.axis_index("f")
    seq = 2 * lax.axis_index("q") + lax.axis_index("c")
    where = jnp.stack([plane, seq]).astype(jnp.int32)
    count, width = tokens.shape
    length = count * seqs
    part = width // seqs
    heads = part // HEAD
    rows = w_qkv.shape[0]
    expert_count = w_router.shape[1]
    own_experts, _ = w_gate.shape[:2]
    slice_ff = w_down.shape[1]
    cut = own_experts * slice_ff

    columns = w_qkv.reshape(rows, 3, seqs, part).transpose(2, 0, 1, 3).reshape(seqs, rows, 3 * part)
    router_wide = jnp.pad(w_router, ((0, 0), (0, LANES - expert_count)))
    columns = jnp.concatenate(
        [columns, jnp.broadcast_to(router_wide, (seqs, rows, LANES))], axis=2
    )
    columns = lax.all_to_all(columns, SEQ, split_axis=0, concat_axis=0, tiled=True)

    mask = jnp.sum(
        (routes[:, :, None] == jnp.arange(expert_count, dtype=jnp.int32)[None, None, :]).astype(F32),
        axis=1,
    )
    wide = jnp.concatenate(
        [cotangent, jnp.pad(mask, ((0, 0), (0, LANES - expert_count))).astype(BF16)], axis=1
    )
    dy_z = jnp.concatenate([swap(wide, "f", planes, k) for k in range(1, planes)], axis=0)

    inputs = tokens.astype(F32)
    in_scale = lax.rsqrt(jnp.mean(inputs * inputs, axis=-1, keepdims=True) + epsilon)
    normed_own = (inputs * in_scale * gains[0]).astype(BF16)
    near, far = seq_gather(after(normed_own, columns), chips)
    normed_attn = jnp.concatenate([near, far], axis=0)
    dy_far = [dy_z] + [swap(dy_z, "q", chips, k) for k in range(1, chips)]
    dy_near = [wide] + [swap(wide, "q", chips, k) for k in range(1, chips)]

    columns = columns.reshape(seqs * rows, 3 * part + LANES)
    columns, out_own, router_own, _ = lax.optimization_barrier(
        (columns[:, : 3 * part], w_out, columns[:, 3 * part :], dy_z)
    )
    qkv_part = lax.all_gather(columns, "f", axis=0, tiled=True)
    out_z = jnp.stack([out_own] + [swap(out_own, "f", planes, k) for k in range(1, planes)])
    router = [router_own] + [swap(router_own, "f", planes, k) for k in range(1, planes)]
    router = by_bits(jnp.stack(router), plane, 0).reshape(width, LANES)

    half = seqs // 2
    lanes = seqs // planes
    b_of = seq % half
    here_f = seq // lanes
    blocks = []
    for j in range(planes):
        pairs = [
            (half * s + (f - j) % planes, lanes * f + s) for f in range(planes) for s in range(lanes)
        ]
        block = lax.dynamic_index_in_dim(
            out_z, ((b_of + j) % planes) ^ plane, 0, keepdims=False
        )
        blocks.append(lax.ppermute(block, SEQ, pairs))
    order = (here_f - jnp.arange(planes)) % planes
    out_rows = jnp.take(jnp.stack(blocks), order, axis=0).reshape(part, width)

    packed = pack_experts(where, w_gate, w_up, planes)
    qkv_part, router, *packed = lax.optimization_barrier((qkv_part, router, *packed))
    arrived = [packed[0]] + [swap(packed[k], "f", planes, k) for k in range(1, planes)]
    own_gu = place_rows(where, arrived)
    other_gu = swap(own_gu, "c", 2, 1)
    own_down = w_down.reshape(cut, width)
    other_down = swap(own_down, "c", 2, 1)

    exponent_index = jnp.arange(HEAD // 2, dtype=F32) * (2.0 / HEAD)
    angles = jnp.arange(length, dtype=F32)[:, None] * (rotary_base ** (-exponent_index))[None, :]
    cosine, sine = jnp.cos(angles), jnp.sin(angles)
    cosine = jnp.concatenate([cosine, cosine], axis=1)
    sine = jnp.concatenate([-sine, sine], axis=1)
    cosine, sine = lax.optimization_barrier((cosine, sine))

    projected = mm(normed_attn, qkv_part, 1, 0)
    queries, keys = projected[:, :part], projected[:, part : 2 * part]
    squares = jnp.stack([jnp.sum(queries * queries, axis=1), jnp.sum(keys * keys, axis=1)])
    scales = lax.rsqrt(small_sum(squares, seq, chips) / width + epsilon)
    gain_rows = lax.dynamic_slice_in_dim(gains[1:3], seq * part, part, axis=1)
    attended, ql, kl, vl, lse = attend(
        where, projected, scales.T, gain_rows, cosine, sine, seqs, heads
    )
    group = chips * count
    out_other = mm(attended[group:], out_rows, 1, 0).astype(BF16)
    out_own = mm(attended[:group], out_rows, 1, 0)
    own, parts = seq_parts(out_own, out_other, chips)
    gain_ffn = gains[3:4]
    residual, normed_low = norm_ffn(tokens, own, parts, gain_ffn)

    x_blocks = []
    for f in range(planes):
        block = normed_low
        if f:
            block = swap(normed_low, "f", planes, f)
        x_blocks.append([block] + [swap(block, "q", chips, k) for k in range(1, chips)])

    acts, grads, outs, back_parts = [], [], None, []
    tight = planes * chips > 16
    for f in range(planes):
        if tight and f > 1:
            x_blocks[f][0] = after(x_blocks[f][0], back_parts[-1])
        if f == 0:
            ys = [(y, 0) for y in dy_near]
        else:
            ys = [(y, f - 1) for y in dy_far]
        results = moe_rows(
            where,
            f,
            planes,
            x_blocks[f],
            ys,
            router,
            [own_gu, other_gu],
            [own_down, other_down],
            outs,
            expert_count,
            own_experts,
        )
        dxs, outs = results[:chips], results[chips : 2 * chips]
        acts.append(results[2 * chips])
        grads.append(results[2 * chips + 1])
        arrivals = [dxs[0]] + [swap(dxs[k], "q", chips, k) for k in range(1, chips)]
        if f:
            total = sum(a.astype(F32) for a in arrivals).astype(BF16)
            arrivals = [swap(total, "f", planes, f)]
        back_parts += arrivals

    groups = max(planes // 2, 1)
    block = groups * count
    total = residual
    for g in reversed(range(planes // groups)):
        moe = outs[0][g * block : (g + 1) * block].astype(F32)
        for k in reversed(range(1, chips)):
            piece = swap(outs[k][g * block : (g + 1) * block], "q", chips, k)
            moe = moe + piece.astype(F32)
        for k in range(g * groups, (g + 1) * groups):
            piece = moe[(k % groups) * count : (k % groups + 1) * count]
            if k:
                piece = swap(piece.astype(BF16), "f", planes, k).astype(F32)
            total = total + piece
    output = total.astype(BF16)

    x_flat = [block for group_blocks in x_blocks for block in group_blocks]
    own_part, other_part = grad_in(where, x_flat, grads)
    other_part = swap(other_part, "c", 2, 1)
    back = merge_parts(where, own_part, other_part, planes)
    back = [back[0]] + [swap(back[k], "f", planes, k) for k in range(1, planes)]
    grad_gate, grad_up = unpack_experts(where, back, own_experts)
    places = [[k] for k in range(chips)]
    places += [[f * chips + k for f in range(1, planes)] for k in range(chips)]
    down_own, down_other = grad_down_rows(where, dy_near + dy_far, places, acts, width, own_experts)
    down_other = swap(down_other, "c", 2, 1)
    grad_down = (down_own + down_other.astype(F32)).reshape(own_experts, slice_ff, width)

    if tight:
        back_parts[0] = after(back_parts[0], output, down_other, *back)

    res_grad, res_low, logit_wide, gain3 = norm_back(
        normed_low, residual, router, wide, gain_ffn, back_parts, expert_count
    )

    res_near, res_far = seq_gather(res_low, chips)
    attended_grad = jnp.concatenate(
        [mm(res_near, out_rows, 1, 1), mm(res_far, out_rows, 1, 1)], axis=0
    ).astype(BF16)
    query_back, key_back, value_low = attend_back(
        where, ql, kl, vl, lse, attended_grad, cosine, sine, seqs, heads
    )
    query_gg, key_gg = query_back * gain_rows[0], key_back * gain_rows[1]
    dots = jnp.stack([jnp.sum(queries * query_gg, axis=1), jnp.sum(keys * key_gg, axis=1)])
    value_term = mm(normed_attn, value_low, 0, 0).astype(BF16)
    value_term, dots = lax.optimization_barrier((value_term, dots))
    value_term = lax.psum_scatter(value_term, "f", scatter_dimension=0, tiled=True)
    scales = from_position(scales, seq, chips).T
    query_scale, key_scale = scales[:, 0:1], scales[:, 1:2]
    gain1 = jnp.sum(query_back * queries * query_scale, axis=0)
    gain2 = jnp.sum(key_back * keys * key_scale, axis=0)
    dots, gain_qk = small_sum(dots, seq, chips, jnp.stack([gain1, gain2]))
    dots = from_position(dots / width, seq, chips).T
    query_pre = query_gg * query_scale - queries * (query_scale**3 * dots[:, 0:1])
    key_pre = key_gg * key_scale - keys * (key_scale**3 * dots[:, 1:2])
    pre_low = jnp.concatenate([query_pre.astype(BF16), key_pre.astype(BF16)], axis=1)
    qk_term = mm(normed_attn, pre_low, 0, 0).astype(BF16)
    qk_term = lax.psum_scatter(qk_term, "f", scatter_dimension=0, tiled=True)
    projected_grad = jnp.concatenate([pre_low, value_low], axis=1)
    back_other = mm(projected_grad[group:], qkv_part, 1, 1).astype(BF16)
    back_own = mm(projected_grad[:group], qkv_part, 1, 1)
    own, parts = seq_parts(back_own, back_other, chips)
    attn_back = own + sum(p.astype(F32) for p in parts)
    scaled = attn_back * gains[0]
    grad_tokens = res_grad + (
        scaled * in_scale - inputs * in_scale**3 * jnp.mean(inputs * scaled, axis=-1, keepdims=True)
    )

    attended_both = attended
    res_both = jnp.concatenate([res_near, res_far], axis=0)
    out_term = mm(attended_both, res_both, 0, 0).astype(BF16).reshape(planes, rows, width)
    pieces = []
    for j in range(planes):
        pairs = [
            (lanes * f + s, half * s + (f - j) % planes) for f in range(planes) for s in range(lanes)
        ]
        block = lax.dynamic_index_in_dim(out_term, (here_f - j) % planes, 0, keepdims=False)
        pieces.append(lax.ppermute(block, SEQ, pairs))
    pieces = jnp.stack(pieces)
    grad_out = jnp.zeros((rows, width), F32)
    for k in range(planes):
        piece = lax.dynamic_index_in_dim(pieces, ((plane ^ k) - b_of) % planes, 0, keepdims=False)
        if k:
            piece = swap(piece, "f", planes, k)
        grad_out = grad_out + piece.astype(F32)

    gain3 = gain3[0]
    gain_high = gain3.astype(BF16)
    gain_low = (gain3 - gain_high.astype(F32)).astype(BF16)
    extra = jnp.concatenate(
        [logit_wide, gain_high.reshape(-1, LANES), gain_low.reshape(-1, LANES)], axis=0
    )
    extras = [extra] + [swap(extra, "q", chips, k) for k in range(1, chips)]
    logit_near = jnp.concatenate([e[:count] for e in extras], axis=0)
    x_near = jnp.concatenate(x_blocks[0], axis=0)
    router_term = mm(x_near, logit_near, 0, 0)
    gain_term = sum(e[count:].astype(F32) for e in extras)
    gain_term = jnp.sum(gain_term.reshape(2, width), axis=0)
    small = jnp.concatenate(
        [router_term[:, :expert_count], gain_term[:, None]], axis=1
    ).reshape(planes, seqs, rows, expert_count + 1)
    small_own = lax.dynamic_index_in_dim(small, seq, 1, keepdims=False)
    small_other = lax.dynamic_index_in_dim(small, seq ^ 1, 1, keepdims=False)
    small_own = small_own + swap(small_other, "c", 2, 1)
    small_sum_z = lax.dynamic_index_in_dim(small_own, plane, 0, keepdims=False)
    for k in range(1, planes):
        small_sum_z = small_sum_z + swap(
            lax.dynamic_index_in_dim(small_own, plane ^ k, 0, keepdims=False), "f", planes, k
        )
    grad_router = small_sum_z[:, :expert_count]

    back_qkv = jnp.concatenate([qk_term, value_term], axis=1).reshape(seqs, rows, 3 * part)
    grad_qkv = lax.all_to_all(back_qkv, SEQ, split_axis=0, concat_axis=0, tiled=True)
    grad_qkv = (
        grad_qkv.reshape(seqs, rows, 3, part)
        .transpose(1, 2, 0, 3)
        .reshape(rows, 3 * width)
        .astype(F32)
    )
    gain_qk = gain_qk.reshape(seqs, 2, part).swapaxes(0, 1)
    gain_qk = lax.dynamic_index_in_dim(gain_qk.reshape(2, planes, seqs, rows), seq, 2, keepdims=False)
    gain_sum = lax.dynamic_index_in_dim(gain_qk, plane, 1, keepdims=False)
    for k in range(1, planes):
        gain_sum = gain_sum + swap(
            lax.dynamic_index_in_dim(gain_qk, plane ^ k, 1, keepdims=False), "f", planes, k
        )
    own_gain = lax.dynamic_slice_in_dim(gains[0], (plane * seqs + seq) * rows, rows)
    gain0 = jnp.sum(w_qkv.astype(F32) * grad_qkv, axis=1) / own_gain
    grad_gains = jnp.concatenate(
        [gain0[None], gain_sum, small_sum_z[:, expert_count][None]], axis=0
    )
    return (
        output,
        grad_tokens,
        grad_gains,
        grad_qkv,
        grad_out,
        grad_router,
        grad_gate,
        grad_up,
        grad_down,
    )


def solution(mesh):
    devices = mesh.devices
    inner = Mesh(devices.reshape(devices.shape[0], devices.shape[1] // 2, 2), ("f", "q", "c"))
    all_axes = ("f", "q", "c")
    by_rows = P(all_axes, None)
    expert = P(SEQ, "f", None)

    return jax.shard_map(
        shards,
        mesh=inner,
        in_specs=(by_rows, by_rows, P(), by_rows, by_rows, by_rows, expert, expert, expert, by_rows),
        out_specs=(
            by_rows,
            by_rows,
            P(None, all_axes),
            by_rows,
            by_rows,
            by_rows,
            expert,
            expert,
            expert,
        ),
        check_vma=False,
    )
```

```python
import functools

import jax
import jax.numpy as jnp
from jax import lax
from jax.experimental import pallas as pl
from jax.experimental.pallas import tpu as pltpu
from jax.sharding import Mesh, PartitionSpec as P


HEAD = 128
LANES = 128

BF16 = jnp.bfloat16
F32 = jnp.float32

epsilon = 1e-05
rotary_base = 10000.0

SEQ = ("q", "c")


def mm(a, b, ca, cb):
    return lax.dot_general(a, b, (((ca,), (cb,)), ((), ())), preferred_element_type=F32)


def swap(value, axis, count, k):
    return lax.ppermute(value, axis, [(i, i ^ k) for i in range(count)])


def after(value, *others):
    return lax.optimization_barrier((value, *others))[0]


def vmem_params(count):
    return pltpu.CompilerParams(
        dimension_semantics=("arbitrary",) * count, vmem_limit_bytes=60 * 1024 * 1024
    )


def held(shape, index_map):
    return pl.BlockSpec(shape, index_map, pipeline_mode=pl.Buffered(1))


def cost(flops, nbytes):
    return pl.CostEstimate(flops=int(flops), bytes_accessed=int(nbytes), transcendentals=0)


def pack_kernel(where, gate_ref, up_ref, *out_refs):
    planes = len(out_refs)
    size = gate_ref.shape[2] // planes
    for k in range(planes):
        columns = pl.ds(pl.multiple_of((where[0] ^ k) * size, 128), size)
        out_refs[k][:, :size] = gate_ref[0, :, columns]
        out_refs[k][:, size:] = up_ref[0, :, columns]


def pack_experts(where, w_gate, w_up, planes):
    experts, slab, full = w_gate.shape
    size = full // planes
    spec = pl.BlockSpec((1, slab, full), lambda e, s: (e, 0, 0))
    out = pl.BlockSpec((slab, 2 * size), lambda e, s: (0, e))
    return pl.pallas_call(
        pack_kernel,
        grid_spec=pltpu.PrefetchScalarGridSpec(
            num_scalar_prefetch=1, grid=(experts,), in_specs=[spec, spec], out_specs=[out] * planes
        ),
        out_shape=[jax.ShapeDtypeStruct((slab, 2 * experts * size), BF16)] * planes,
        compiler_params=vmem_params(1),
        name="pack_experts",
    )(where, w_gate, w_up)


def place_kernel(where, *refs):
    out_ref = refs[-1]
    for k, piece in enumerate(refs[:-1]):
        size = piece.shape[0]
        out_ref[pl.ds(pl.multiple_of((where[0] ^ k) * size, 128), size), :] = piece[...]


def place_rows(where, pieces):
    rows, columns = pieces[0].shape
    full = rows * len(pieces)
    half = columns // 2
    return pl.pallas_call(
        place_kernel,
        grid_spec=pltpu.PrefetchScalarGridSpec(
            num_scalar_prefetch=1,
            grid=(2,),
            in_specs=[pl.BlockSpec((rows, half), lambda i, s: (0, i))] * len(pieces),
            out_specs=pl.BlockSpec((full, half), lambda i, s: (0, i)),
        ),
        out_shape=jax.ShapeDtypeStruct((full, columns), BF16),
        compiler_params=vmem_params(1),
        name="place_rows",
    )(where, *pieces)


def unpack_kernel(where, *refs):
    gate_ref, up_ref = refs[-2:]
    size = refs[0].shape[1] // 2
    for k, piece in enumerate(refs[:-2]):
        columns = pl.ds(pl.multiple_of((where[0] ^ k) * size, 128), size)
        gate_ref[0, :, columns] = piece[:, :size].astype(F32)
        up_ref[0, :, columns] = piece[:, size:].astype(F32)


def unpack_experts(where, pieces, experts):
    slab, columns = pieces[0].shape
    size = columns // (2 * experts)
    full = size * len(pieces)
    spec = pl.BlockSpec((slab, 2 * size), lambda e, s: (0, e))
    out = pl.BlockSpec((1, slab, full), lambda e, s: (e, 0, 0))
    shape = jax.ShapeDtypeStruct((experts, slab, full), F32)
    return pl.pallas_call(
        unpack_kernel,
        grid_spec=pltpu.PrefetchScalarGridSpec(
            num_scalar_prefetch=1,
            grid=(experts,),
            in_specs=[spec] * len(pieces),
            out_specs=[out, out],
        ),
        out_shape=[shape, shape],
        compiler_params=vmem_params(1),
        name="unpack_experts",
    )(where, *pieces)


def moe_kernel(count, experts, own_experts, aliased, where, *refs):
    x_refs, y_refs = refs[:count], refs[count : 2 * count]
    router_ref = refs[2 * count]
    gu_refs, down_refs = refs[2 * count + 1 : 2 * count + 3], refs[2 * count + 3 : 2 * count + 5]
    refs = refs[2 * count + 5 + (count if aliased else 0) :]
    dx_refs, out_refs = refs[:count], refs[count : 2 * count]
    act_ref, grad_ref = refs[2 * count : 2 * count + 2]
    xs, ys, gu_all, down_all, prob_sum, sems = refs[2 * count + 2 :]
    rows, width = x_refs[0].shape
    steps, size = down_all.shape[:2]

    for e in range(steps):
        side, i = divmod(e, own_experts)
        cols = slice(i * 2 * size, (i + 1) * 2 * size)
        lines = slice(i * size, (i + 1) * size)
        pltpu.make_async_copy(gu_refs[side].at[:, cols], gu_all.at[e], sems.at[0, e]).start()
        pltpu.make_async_copy(down_refs[side].at[lines, :], down_all.at[e], sems.at[1, e]).start()
    for i in range(count):
        here = slice(i * rows, (i + 1) * rows)
        xs[here, :] = x_refs[i][...]
        ys[here, :] = y_refs[i][:, :width]
    logits = mm(xs[...], router_ref[...], 1, 0)
    lane = lax.broadcasted_iota(jnp.int32, logits.shape, 1)
    logits = jnp.where(lane < experts, logits, -jnp.inf)
    spread = jnp.exp(logits - jnp.max(logits, axis=1, keepdims=True))
    probs = spread / jnp.sum(spread, axis=1, keepdims=True)
    weight = probs * jnp.concatenate([y[:, width:].astype(F32) for y in y_refs], axis=0)
    prob_sum[...] = jnp.zeros_like(prob_sum)

    def one_expert(e, carry):
        pltpu.make_async_copy(gu_all.at[e], gu_all.at[e], sems.at[0, e]).wait()
        pltpu.make_async_copy(down_all.at[e], down_all.at[e], sems.at[1, e]).wait()
        which = jnp.where(
            e < own_experts,
            where[1] * own_experts + e,
            (where[1] ^ 1) * own_experts + e - own_experts,
        )
        prob = jnp.sum(jnp.where(lane == which, weight, 0.0), axis=1, keepdims=True)
        both = mm(xs[...], gu_all[e], 1, 0)
        gate, up = both[:, :size], both[:, size:]
        sig = 1.0 / (1.0 + jnp.exp(-gate))
        back = mm(ys[...], down_all[e], 1, 1)
        silu = gate * sig
        act = silu * up
        prob_sum[...] += jnp.where(lane == which, jnp.sum(act * back, axis=1, keepdims=True), 0.0)
        back = back * prob
        act_ref[:, pl.ds(pl.multiple_of(e * size, size), size)] = (act * prob).astype(BF16)
        grad_ref[:, pl.ds(pl.multiple_of(2 * e * size, size), size)] = (
            back * up * sig * (1.0 + gate * (1.0 - sig))
        ).astype(BF16)
        grad_ref[:, pl.ds(pl.multiple_of((2 * e + 1) * size, size), size)] = (back * silu).astype(
            BF16
        )
        return carry

    lax.fori_loop(0, steps, one_expert, 0)
    tile = min(512, width)

    def one_tile(n, carry):
        cols = pl.ds(pl.multiple_of(n * tile, tile), tile)
        dx = out = None
        for e in range(steps):
            term = mm(grad_ref[:, 2 * e * size : 2 * (e + 1) * size], gu_all[e, cols, :], 1, 1)
            dx = term if dx is None else dx + term
            term = mm(act_ref[:, e * size : (e + 1) * size], down_all[e, :, cols], 1, 0)
            out = term if out is None else out + term
        for i in range(count):
            here = slice(i * rows, (i + 1) * rows)
            dx_refs[i][:, cols] = dx[here].astype(BF16)
            out_refs[i][:, cols] = out[here].astype(BF16)
        return carry

    lax.fori_loop(0, width // tile, one_tile, 0)
    for i in range(count):
        dx_refs[i][:, width:] = prob_sum[i * rows : (i + 1) * rows].astype(BF16)


def moe_rows(where, group, groups, xs, ys, router, gus, downs, outs, experts, own_experts):
    count = len(xs)
    rows, width = xs[0].shape
    size = downs[0].shape[0] // own_experts
    total = count * rows
    steps = 2 * own_experts
    lanes = router.shape[1]
    aliased = outs is not None

    def fixed(block):
        return lambda i, s: (block, 0)

    anywhere = pl.BlockSpec(memory_space=pl.ANY)
    in_specs = (
        [held((rows, width), fixed(0)) for _ in xs]
        + [held((rows, y.shape[1]), fixed(i)) for y, i in ys]
        + [held(router.shape, fixed(0))]
        + [anywhere] * 4
        + ([anywhere] * count if aliased else [])
    )
    out_specs = (
        [held((rows, width + lanes), fixed(0))] * count
        + [held((rows, width), fixed(group))] * count
        + [held((total, steps * size), fixed(0)), held((total, 2 * steps * size), fixed(0))]
    )
    first = 1 + 2 * count + 5
    return pl.pallas_call(
        functools.partial(moe_kernel, count, experts, own_experts, aliased),
        grid_spec=pltpu.PrefetchScalarGridSpec(
            num_scalar_prefetch=1,
            grid=(1,),
            in_specs=in_specs,
            out_specs=out_specs,
            scratch_shapes=[
                pltpu.VMEM((total, width), BF16),
                pltpu.VMEM((total, width), BF16),
                pltpu.VMEM((steps, width, 2 * size), BF16),
                pltpu.VMEM((steps, size, width), BF16),
                pltpu.VMEM((total, lanes), F32),
                pltpu.SemaphoreType.DMA((2, steps)),
            ],
        ),
        out_shape=[jax.ShapeDtypeStruct((rows, width + lanes), BF16)] * count
        + [jax.ShapeDtypeStruct((groups * rows, width), BF16)] * count
        + [
            jax.ShapeDtypeStruct((total, steps * size), BF16),
            jax.ShapeDtypeStruct((total, 2 * steps * size), BF16),
        ],
        input_output_aliases={first + i: count + i for i in range(count)} if aliased else {},
        compiler_params=vmem_params(1),
        cost_estimate=cost(
            12 * total * width * size * steps, 8 * total * width + 6 * width * size * steps
        ),
        name="moe_rows",
    )(where, *xs, *[y for y, _ in ys], router, *gus, *downs, *(outs or []))


def norm_ffn_kernel(token_ref, own_ref, *refs):
    gain_ref, res_ref, low_ref = refs[-3:]
    total = token_ref[...].astype(F32) + own_ref[...]
    for ref in refs[:-3]:
        total = total + ref[...].astype(F32)
    res_ref[...] = total
    scale = lax.rsqrt(jnp.mean(total * total, axis=1, keepdims=True) + epsilon)
    low_ref[...] = (total * scale * gain_ref[...]).astype(BF16)


def norm_ffn(tokens, own, parts, gain):
    return pl.pallas_call(
        norm_ffn_kernel,
        out_shape=[
            jax.ShapeDtypeStruct(tokens.shape, F32),
            jax.ShapeDtypeStruct(tokens.shape, BF16),
        ],
        compiler_params=vmem_params(0),
        cost_estimate=cost(10 * tokens.size, 16 * tokens.size),
        name="norm_ffn",
    )(tokens, own, *parts, gain)


def norm_back_kernel(experts, low_ref, res_ref, router_ref, wide_ref, gain_ref, *refs):
    grad_ref, grad_low_ref, logit_ref, gain_out = refs[-4:]
    width = res_ref.shape[1]
    total = refs[0][...].astype(F32)
    for ref in refs[1:-4]:
        total = total + ref[...].astype(F32)
    upstream = wide_ref[:, :width].astype(F32)
    mask = wide_ref[:, width:].astype(F32)
    logits = mm(low_ref[...], router_ref[...], 1, 0)
    lane = lax.broadcasted_iota(jnp.int32, logits.shape, 1)
    logits = jnp.where(lane < experts, logits, -jnp.inf)
    spread = jnp.exp(logits - jnp.max(logits, axis=1, keepdims=True))
    probs = spread / jnp.sum(spread, axis=1, keepdims=True)
    prob_full = total[:, width:] * mask
    logit = (
        probs * (prob_full - jnp.sum(probs * prob_full, axis=1, keepdims=True))
    ).astype(BF16)
    logit_ref[...] = logit
    dn = total[:, :width] + mm(logit, router_ref[...], 1, 1)
    residual = res_ref[...]
    scale = lax.rsqrt(jnp.mean(residual * residual, axis=1, keepdims=True) + epsilon)
    scaled = dn * gain_ref[...]
    grad = upstream + (
        scaled * scale - residual * (scale**3 * jnp.mean(residual * scaled, axis=1, keepdims=True))
    )
    grad_ref[...] = grad
    grad_low_ref[...] = grad.astype(BF16)
    gain_out[...] = jnp.sum(dn * residual * scale, axis=0, keepdims=True)


def norm_back(low, residual, router, wide, gain, parts, experts):
    count, width = residual.shape
    return pl.pallas_call(
        functools.partial(norm_back_kernel, experts),
        out_shape=[
            jax.ShapeDtypeStruct((count, width), F32),
            jax.ShapeDtypeStruct((count, width), BF16),
            jax.ShapeDtypeStruct((count, router.shape[1]), BF16),
            jax.ShapeDtypeStruct((1, width), F32),
        ],
        compiler_params=vmem_params(0),
        cost_estimate=cost(20 * low.size, 30 * low.size),
        name="norm_back",
    )(low, residual, router, wide, gain, *parts)


def merge_kernel(planes, where, own_ref, other_ref, *out_refs):
    total = own_ref[...].astype(F32) + other_ref[...].astype(F32)
    k = pl.program_id(0)
    for i in range(planes):

        @pl.when(k == i)
        def _(i=i):
            out_refs[i][...] = total.astype(BF16)


def merge_parts(where, own, other, planes):
    slab, columns = own.shape[0] // planes, own.shape[1]
    spec = pl.BlockSpec((slab, columns), lambda k, s: (s[0] ^ k, 0))
    return pl.pallas_call(
        functools.partial(merge_kernel, planes),
        grid_spec=pltpu.PrefetchScalarGridSpec(
            num_scalar_prefetch=1,
            grid=(planes,),
            in_specs=[spec, spec],
            out_specs=[pl.BlockSpec((slab, columns), lambda k, s: (0, 0))] * planes,
        ),
        out_shape=[jax.ShapeDtypeStruct((slab, columns), BF16)] * planes,
        compiler_params=vmem_params(1),
        cost_estimate=cost(own.size, 6 * own.size),
        name="merge_parts",
    )(where, own, other)


def grad_in_kernel(groups, count, where, *refs):
    x_refs = refs[: groups * count]
    g_refs = refs[groups * count : groups * count + groups]
    own_ref, other_ref, xs = refs[groups * count + groups :]
    rows = x_refs[0].shape[0]
    half = own_ref.shape[1]
    for i, x in enumerate(x_refs):
        xs[i * rows : (i + 1) * rows, :] = x[...]
    step = count * rows
    for out, start in ((own_ref, 0), (other_ref, half)):
        total = None
        for g in range(groups):
            term = mm(
                xs[g * step : (g + 1) * step, :], g_refs[g][:, start : start + half], 0, 0
            )
            total = term if total is None else total + term
        out[...] = total.astype(BF16)


def grad_in(where, xs, grads, tile=256):
    groups, count = len(grads), len(xs) // len(grads)
    rows, width = xs[0].shape
    columns = grads[0].shape[1]
    shape = jax.ShapeDtypeStruct((width, columns // 2), BF16)
    return pl.pallas_call(
        functools.partial(grad_in_kernel, groups, count),
        grid_spec=pltpu.PrefetchScalarGridSpec(
            num_scalar_prefetch=1,
            grid=(width // tile,),
            in_specs=[pl.BlockSpec((rows, tile), lambda i, s: (0, i))] * len(xs)
            + [held(g.shape, lambda i, s: (0, 0)) for g in grads],
            out_specs=[pl.BlockSpec((tile, columns // 2), lambda i, s: (i, 0))] * 2,
            scratch_shapes=[pltpu.VMEM((rows * len(xs), tile), BF16)],
        ),
        out_shape=[shape, shape],
        compiler_params=vmem_params(1),
        cost_estimate=cost(
            2 * rows * len(xs) * width * columns, 2 * rows * len(xs) * (width + columns)
        ),
        name="grad_in",
    )(where, *xs, *grads)


def grad_down_kernel(places, own_steps, where, *refs):
    y_refs = refs[: len(places)]
    groups = len(refs) - len(places) - 3
    a_refs = refs[len(places) : len(places) + groups]
    own_ref, other_ref, ys = refs[len(places) + groups :]
    e = pl.program_id(1)

    @pl.when(e == 0)
    def _():
        for ref, there in zip(y_refs, places):
            size = ref.shape[0] // len(there)
            for i, place in enumerate(there):
                ys[place * size : (place + 1) * size, :] = ref[i * size : (i + 1) * size, :]

    step = a_refs[0].shape[0]
    total = None
    for g in range(groups):
        term = mm(a_refs[g][...], ys[g * step : (g + 1) * step, :], 0, 0)
        total = term if total is None else total + term

    @pl.when(e < own_steps)
    def _():
        own_ref[...] = total

    @pl.when(e >= own_steps)
    def _():
        other_ref[...] = total.astype(BF16)


def grad_down_rows(where, ys, places, acts, width, own_experts):
    size = acts[0].shape[1] // (2 * own_experts)
    last = own_experts - 1
    total = acts[0].shape[0] * len(acts)
    tile = width
    while total * tile > 1 << 21:
        tile //= 2
    return pl.pallas_call(
        functools.partial(grad_down_kernel, places, own_experts),
        grid_spec=pltpu.PrefetchScalarGridSpec(
            num_scalar_prefetch=1,
            grid=(width // tile, 2 * own_experts),
            in_specs=[pl.BlockSpec((y.shape[0], tile), lambda j, e, s: (0, j)) for y in ys]
            + [pl.BlockSpec((a.shape[0], size), lambda j, e, s: (0, e)) for a in acts],
            out_specs=[
                pl.BlockSpec((size, tile), lambda j, e, s: (jnp.minimum(e, last), j)),
                pl.BlockSpec((size, tile), lambda j, e, s: (jnp.maximum(e - own_experts, 0), j)),
            ],
            scratch_shapes=[pltpu.VMEM((total, tile), BF16)],
        ),
        out_shape=[
            jax.ShapeDtypeStruct((own_experts * size, width), F32),
            jax.ShapeDtypeStruct((own_experts * size, width), BF16),
        ],
        compiler_params=vmem_params(2),
        cost_estimate=cost(
            4 * total * width * size * own_experts, 2 * total * (width + 2 * size * own_experts)
        ),
        name="grad_down_rows",
    )(where, *ys, *acts)


def block_rows(seq, block, seqs, size):
    k = seq ^ block
    return pl.ds(pl.multiple_of(((k & 1) * (seqs // 2) + (k >> 1)) * size, size), size)


def turned(values, cosine, sine):
    return values * cosine + pltpu.roll(values, values.shape[1] // 2, 1) * sine


def attend_kernel(seqs, tile, where, q_ref, k_ref, v_ref, scale_ref, gain_ref, cos_ref, sin_ref, att_ref, ql, kl, vl, lse_ref):
    length, head = q_ref.shape
    size = length // seqs
    for b in range(seqs):
        rows = block_rows(where[1], b, seqs, size)
        here = slice(b * size, (b + 1) * size)
        cosine, sine = cos_ref[here, :], sin_ref[here, :]
        scales = scale_ref[here, :]
        ql[here, :] = turned(
            q_ref[rows, :] * scales[:, 0:1] * gain_ref[0:1, :], cosine, sine
        ).astype(BF16)
        kl[here, :] = turned(
            k_ref[rows, :] * scales[:, 1:2] * gain_ref[1:2, :], cosine, sine
        ).astype(BF16)
        vl[here, :] = v_ref[rows, :].astype(BF16)
    diagonal = lax.broadcasted_iota(jnp.int32, (tile, tile), 0) >= lax.broadcasted_iota(
        jnp.int32, (tile, tile), 1
    )
    for t in range(length // tile):
        here = slice(t * tile, (t + 1) * tile)
        limit = (t + 1) * tile
        scores = mm(ql[here, :], kl[:limit, :], 1, 1) * (head ** (-0.5))
        edge = jnp.where(diagonal, scores[:, t * tile :], -jnp.inf)
        scores = jnp.concatenate([scores[:, : t * tile], edge], axis=1) if t else edge
        peak = jnp.max(scores, axis=1, keepdims=True)
        spread = jnp.exp(scores - peak)
        total = jnp.sum(spread, axis=1, keepdims=True)
        weights = (spread * (1.0 / total)).astype(BF16)
        out = mm(weights, vl[:limit, :], 1, 0).astype(BF16)
        lse_ref[here, :] = jnp.broadcast_to(peak + jnp.log(total), (tile, head))
        for b in range(tile // size):
            rows = block_rows(where[1], t * (tile // size) + b, seqs, size)
            att_ref[rows, :] = out[b * size : (b + 1) * size]


def attend(where, projected, scales, gain_rows, cosine, sine, seqs, heads, tile=256):
    length = projected.shape[0]
    head = projected.shape[1] // (3 * heads)
    part = heads * head

    def column(offset):
        return pl.BlockSpec((length, head), lambda h, s: (0, offset + h))

    full = pl.BlockSpec((length, head), lambda h, s: (0, 0))
    low = jax.ShapeDtypeStruct((length, part), BF16)
    return pl.pallas_call(
        functools.partial(attend_kernel, seqs, tile),
        grid_spec=pltpu.PrefetchScalarGridSpec(
            num_scalar_prefetch=1,
            grid=(heads,),
            in_specs=[
                column(0),
                column(heads),
                column(2 * heads),
                pl.BlockSpec(scales.shape, lambda h, s: (0, 0)),
                pl.BlockSpec((2, head), lambda h, s: (0, h)),
                full,
                full,
            ],
            out_specs=[column(0)] * 5,
        ),
        out_shape=[low, low, low, low, jax.ShapeDtypeStruct((length, part), F32)],
        compiler_params=vmem_params(1),
        cost_estimate=cost(4 * length * length * part, 20 * length * part),
        name="attend",
    )(where, projected, projected, projected, scales, gain_rows, cosine, sine)


def attend_back_kernel(seqs, tile, where, q_ref, k_ref, v_ref, lse_ref, grad_ref, cos_ref, sin_ref, dq_ref, dk_ref, dv_ref, go, dk, dv):
    length, head = q_ref.shape
    size = length // seqs
    scale = head ** (-0.5)
    for b in range(seqs):
        go[b * size : (b + 1) * size, :] = grad_ref[block_rows(where[1], b, seqs, size), :]
    dk[...] = jnp.zeros_like(dk)
    dv[...] = jnp.zeros_like(dv)
    diagonal = lax.broadcasted_iota(jnp.int32, (tile, tile), 0) >= lax.broadcasted_iota(
        jnp.int32, (tile, tile), 1
    )
    for t in range(length // tile):
        here = slice(t * tile, (t + 1) * tile)
        limit = (t + 1) * tile
        scores = mm(q_ref[here, :], k_ref[:limit, :], 1, 1) * scale
        edge = jnp.where(diagonal, scores[:, t * tile :], -jnp.inf)
        scores = jnp.concatenate([scores[:, : t * tile], edge], axis=1) if t else edge
        probs = jnp.exp(scores - lse_ref[here, 0:1])
        dprobs = mm(go[here, :], v_ref[:limit, :], 1, 1)
        terms = probs * dprobs
        dscores = (terms - probs * jnp.sum(terms, axis=1, keepdims=True)).astype(BF16)
        dq = (mm(dscores, k_ref[:limit, :], 1, 0) * scale).astype(BF16).astype(F32)
        dq = turned(dq, cos_ref[here, :], -sin_ref[here, :])
        for b in range(tile // size):
            rows = block_rows(where[1], t * (tile // size) + b, seqs, size)
            dq_ref[rows, :] = dq[b * size : (b + 1) * size]
        dk[:limit, :] += mm(dscores, q_ref[here, :], 0, 0)
        dv[:limit, :] += mm(probs.astype(BF16), go[here, :], 0, 0)
    for b in range(seqs):
        here = slice(b * size, (b + 1) * size)
        rows = block_rows(where[1], b, seqs, size)
        back = (dk[here, :] * scale).astype(BF16).astype(F32)
        dk_ref[rows, :] = turned(back, cos_ref[here, :], -sin_ref[here, :])
        dv_ref[rows, :] = dv[here, :].astype(BF16)


def attend_back(where, ql, kl, vl, lse, grads, cosine, sine, seqs, heads, tile=256):
    length, part = ql.shape
    head = part // heads
    column = pl.BlockSpec((length, head), lambda h, s: (0, h))
    full = pl.BlockSpec((length, head), lambda h, s: (0, 0))
    wide = jax.ShapeDtypeStruct((length, part), F32)
    return pl.pallas_call(
        functools.partial(attend_back_kernel, seqs, tile),
        grid_spec=pltpu.PrefetchScalarGridSpec(
            num_scalar_prefetch=1,
            grid=(heads,),
            in_specs=[column] * 5 + [full, full],
            out_specs=[column] * 3,
            scratch_shapes=[
                pltpu.VMEM((length, head), BF16),
                pltpu.VMEM((length, head), F32),
                pltpu.VMEM((length, head), F32),
            ],
        ),
        out_shape=[wide, wide, jax.ShapeDtypeStruct((length, part), BF16)],
        compiler_params=vmem_params(1),
        cost_estimate=cost(10 * length * length * part, 24 * length * part),
        name="attend_back",
    )(where, ql, kl, vl, lse, grads, cosine, sine)


def seq_gather(block, chips):
    near = [block] + [swap(block, "q", chips, k) for k in range(1, chips)]
    near = jnp.concatenate(near, axis=0)
    return near, swap(near, "c", 2, 1)


def seq_parts(own, other, chips):
    total = own + swap(other, "c", 2, 1).astype(F32)
    rows = total.shape[0] // chips
    low = total[rows:].astype(BF16)
    parts = [swap(low[(k - 1) * rows : k * rows], "q", chips, k) for k in range(1, chips)]
    return total[:rows], parts


def masks_of(planes):
    return [3, 1] if planes == 4 else [1 << i for i in range(planes.bit_length() - 1)]


def plane_gather(block, planes):
    rows = block.shape[0]
    have, parts = {0: (block, 0)}, [(block, [0])]
    for mask in masks_of(planes):
        keys = [k for _, ks in parts for k in ks]
        sent = parts[0][0] if len(parts) == 1 else jnp.concatenate([a for a, _ in parts], axis=0)
        arrived = swap(sent, "f", planes, mask)
        keys = [k ^ mask for k in keys]
        parts.append((arrived, keys))
        have.update({k: (arrived, j) for j, k in enumerate(keys)})
    return have, parts[1:], rows


def plane_reduce(blocks, planes):
    held_back = dict(enumerate(blocks))
    for i, mask in enumerate(reversed(masks_of(planes))):
        span = {0}
        for other in masks_of(planes)[: len(masks_of(planes)) - 1 - i]:
            span |= {k ^ other for k in span}
        keys = sorted(span)
        sent = jnp.concatenate([held_back[k ^ mask].astype(BF16) for k in keys], axis=0)
        rows = sent.shape[0] // len(keys)
        arrived = swap(sent, "f", planes, mask)
        held_back = {
            k: held_back[k] + arrived[j * rows : (j + 1) * rows].astype(F32)
            for j, k in enumerate(keys)
        }
    return held_back[0]


def by_bits(values, index, axis):
    size = values.shape[axis]
    bit = 1
    while bit < size:
        pieces = [lax.slice_in_dim(values, i, i + bit, axis=axis) for i in range(0, size, bit)]
        turned_over = jnp.concatenate([pieces[i ^ 1] for i in range(len(pieces))], axis=axis)
        values = jnp.where((index & bit) > 0, turned_over, values)
        bit *= 2
    return values


def to_position(values, seq, chips):
    n = values.shape[0]
    values = values.reshape(n, 2, chips, -1)
    values = by_bits(by_bits(values, seq & 1, 1), seq >> 1, 2)
    return values.swapaxes(1, 2).reshape(n, -1)


def from_position(values, seq, chips):
    n = values.shape[0]
    values = values.reshape(n, chips, 2, -1).swapaxes(1, 2)
    return by_bits(by_bits(values, seq & 1, 1), seq >> 1, 2).reshape(n, -1)


def small_sum(pair, seq, chips, rider=None):
    flat = to_position(pair, seq, chips).reshape(-1, LANES)
    count = flat.shape[0]
    if rider is not None:
        flat = jnp.concatenate([flat, rider.reshape(-1, LANES)], axis=0)
    every = lax.all_gather(flat, SEQ, axis=0)
    total = jnp.sum(every[:, :count], axis=0).reshape(pair.shape)
    return total if rider is None else (total, every[:, count:])


def shards(tokens, cotangent, gains, w_qkv, w_out, w_router, w_gate, w_up, w_down, routes):
    planes = lax.axis_size("f")
    chips = lax.axis_size("q")
    seqs = 2 * chips
    plane = lax.axis_index("f")
    seq = 2 * lax.axis_index("q") + lax.axis_index("c")
    where = jnp.stack([plane, seq]).astype(jnp.int32)
    count, width = tokens.shape
    length = count * seqs
    part = width // seqs
    heads = part // HEAD
    rows = w_qkv.shape[0]
    expert_count = w_router.shape[1]
    own_experts, _ = w_gate.shape[:2]
    slice_ff = w_down.shape[1]
    cut = own_experts * slice_ff

    columns = w_qkv.reshape(rows, 3, seqs, part).transpose(2, 0, 1, 3).reshape(seqs, rows, 3 * part)
    router_wide = jnp.pad(w_router, ((0, 0), (0, LANES - expert_count)))
    columns = jnp.concatenate(
        [columns, jnp.broadcast_to(router_wide, (seqs, rows, LANES))], axis=2
    )
    columns = lax.all_to_all(columns, SEQ, split_axis=0, concat_axis=0, tiled=True)

    mask = jnp.sum(
        (routes[:, :, None] == jnp.arange(expert_count, dtype=jnp.int32)[None, None, :]).astype(F32),
        axis=1,
    )
    wide = jnp.concatenate(
        [cotangent, jnp.pad(mask, ((0, 0), (0, LANES - expert_count))).astype(BF16)], axis=1
    )
    _, dy_parts, _ = plane_gather(wide, planes)

    inputs = tokens.astype(F32)
    in_scale = lax.rsqrt(jnp.mean(inputs * inputs, axis=-1, keepdims=True) + epsilon)
    normed_own = (inputs * in_scale * gains[0]).astype(BF16)
    near, far = seq_gather(after(normed_own, columns), chips)
    normed_attn = jnp.concatenate([near, far], axis=0)
    dy_far = []
    for value, there in dy_parts:
        dy_far.append(([value] + [swap(value, "q", chips, k) for k in range(1, chips)], there))
    dy_near = [wide] + [swap(wide, "q", chips, k) for k in range(1, chips)]

    columns = columns.reshape(seqs * rows, 3 * part + LANES)
    router_own = columns[:, 3 * part :]
    columns = after(columns[:, : 3 * part], dy_parts[-1][0])
    qkv_part = lax.all_gather(columns, "f", axis=0, tiled=True)
    nearest = sorted(range(1, planes), key=lambda k: -k if planes == 4 and k == 3 else k)
    out_z, router = {0: w_out}, {0: router_own}
    for k in nearest:
        out_z[k] = swap(w_out, "f", planes, k)
    for k in nearest:
        router[k] = swap(router_own, "f", planes, k)
    out_z = jnp.stack([out_z[k] for k in range(planes)])
    router = jnp.stack([router[k] for k in range(planes)])
    router = by_bits(router, plane, 0).reshape(width, LANES)

    half = seqs // 2
    lanes = seqs // planes
    b_of = seq % half
    here_f = seq // lanes
    blocks = []
    for j in range(planes):
        pairs = [
            (half * s + (f - j) % planes, lanes * f + s) for f in range(planes) for s in range(lanes)
        ]
        block = lax.dynamic_index_in_dim(
            out_z, ((b_of + j) % planes) ^ plane, 0, keepdims=False
        )
        blocks.append(lax.ppermute(block, SEQ, pairs))
    order = (here_f - jnp.arange(planes)) % planes
    out_rows = jnp.take(jnp.stack(blocks), order, axis=0).reshape(part, width)

    packed = pack_experts(where, w_gate, w_up, planes)
    qkv_part, *packed = lax.optimization_barrier((qkv_part, *packed))
    arrived = [packed[0]]
    for k in range(1, planes):
        arrived.append(swap(packed[k], "f", planes, k))
    own_gu = place_rows(where, arrived)
    other_gu = swap(own_gu, "c", 2, 1)
    own_down = w_down.reshape(cut, width)
    other_down = swap(own_down, "c", 2, 1)

    exponent_index = jnp.arange(HEAD // 2, dtype=F32) * (2.0 / HEAD)
    angles = jnp.arange(length, dtype=F32)[:, None] * (rotary_base ** (-exponent_index))[None, :]
    cosine, sine = jnp.cos(angles), jnp.sin(angles)
    cosine = jnp.concatenate([cosine, cosine], axis=1)
    sine = jnp.concatenate([-sine, sine], axis=1)
    cosine, sine = lax.optimization_barrier((cosine, sine))

    projected = mm(normed_attn, qkv_part, 1, 0)
    queries, keys = projected[:, :part], projected[:, part : 2 * part]
    squares = jnp.stack([jnp.sum(queries * queries, axis=1), jnp.sum(keys * keys, axis=1)])
    scales = lax.rsqrt(small_sum(squares, seq, chips) / width + epsilon)
    gain_rows = lax.dynamic_slice_in_dim(gains[1:3], seq * part, part, axis=1)
    attended, ql, kl, vl, lse = attend(
        where, projected, scales.T, gain_rows, cosine, sine, seqs, heads
    )
    group = chips * count
    out_other = mm(attended[group:], out_rows, 1, 0).astype(BF16)
    out_own = mm(attended[:group], out_rows, 1, 0)
    own, parts = seq_parts(out_own, out_other, chips)
    gain_ffn = gains[3:4]
    residual, normed_low = norm_ffn(tokens, own, parts, gain_ffn)

    x_blocks, x_planes = [], {}
    for f in range(planes):
        block = normed_low
        if planes == 4 and f == 2:
            block = swap(x_planes[3], "f", planes, 1)
        elif f:
            block = x_planes[f] if f in x_planes else swap(normed_low, "f", planes, f)
        if planes == 4 and f == 1:
            x_planes[3] = swap(normed_low, "f", planes, 3)
        x_blocks.append([block] + [swap(block, "q", chips, k) for k in range(1, chips)])

    acts, grads, outs, back_parts = [], [], None, []
    tight = planes * chips > 16
    for f in range(planes):
        if tight and f > 1:
            x_blocks[f][0] = after(x_blocks[f][0], back_parts[-1])
        if f == 0:
            ys = [(y, 0) for y in dy_near]
        else:
            ys = [(y, there.index(f)) for some, there in dy_far if f in there for y in some]
        results = moe_rows(
            where,
            f,
            planes,
            x_blocks[f],
            ys,
            router,
            [own_gu, other_gu],
            [own_down, other_down],
            outs,
            expert_count,
            own_experts,
        )
        dxs, outs = results[:chips], results[chips : 2 * chips]
        acts.append(results[2 * chips])
        grads.append(results[2 * chips + 1])
        arrivals = [dxs[0]] + [swap(dxs[k], "q", chips, k) for k in range(1, chips)]
        if f:
            if planes == 4 and f == 3:
                arrivals.append(from_next)
            total = sum(a.astype(F32) for a in arrivals).astype(BF16)
            mask = 1 if planes == 4 and f == 2 else f
            arrivals = [swap(total, "f", planes, mask)]
            if planes == 4 and f == 2:
                from_next, arrivals = arrivals[0], []
        back_parts += arrivals

    groups = max(planes // 2, 1)
    block = groups * count
    total = residual
    for g in reversed(range(planes // groups)):
        pieces = []
        for k in reversed(range(1, chips)):
            pieces.append(swap(outs[k][g * block : (g + 1) * block], "q", chips, k))
        moe = after(outs[0][g * block : (g + 1) * block], *pieces).astype(F32)
        moe = moe + sum(piece.astype(F32) for piece in pieces)
        pieces = [moe[i * count : (i + 1) * count] for i in range(groups)]
        if planes == 4 and g:
            arrived = swap(pieces[0].astype(BF16), "f", planes, 1).astype(F32)
            total = total + swap((pieces[1] + arrived).astype(BF16), "f", planes, 3).astype(F32)
            continue
        for k, piece in enumerate(pieces, g * groups):
            if k:
                piece = swap(piece.astype(BF16), "f", planes, k).astype(F32)
            total = total + piece
    output = total.astype(BF16)

    x_flat = [block for group_blocks in x_blocks for block in group_blocks]
    own_part, other_part = grad_in(where, x_flat, grads)
    other_part = swap(other_part, "c", 2, 1)
    back = list(merge_parts(where, own_part, other_part, planes))
    for k in range(1, planes):
        back[k] = swap(back[k], "f", planes, k)
    grad_gate, grad_up = unpack_experts(where, back, own_experts)
    places = [[k] for k in range(chips)]
    dy_all = list(dy_near)
    for dy_some, there in dy_far:
        dy_all += dy_some
        places += [[f * chips + k for f in there] for k in range(chips)]
    down_own, down_other = grad_down_rows(where, dy_all, places, acts, width, own_experts)
    down_other = swap(down_other, "c", 2, 1)
    grad_down = (down_own + down_other.astype(F32)).reshape(own_experts, slice_ff, width)

    if tight:
        back_parts[0] = after(back_parts[0], output, down_other, *back)

    res_grad, res_low, logit_wide, gain3 = norm_back(
        normed_low, residual, router, wide, gain_ffn, back_parts, expert_count
    )

    res_near, res_far = seq_gather(res_low, chips)
    attended_grad = jnp.concatenate(
        [mm(res_near, out_rows, 1, 1), mm(res_far, out_rows, 1, 1)], axis=0
    ).astype(BF16)
    query_back, key_back, value_low = attend_back(
        where, ql, kl, vl, lse, attended_grad, cosine, sine, seqs, heads
    )
    query_gg, key_gg = query_back * gain_rows[0], key_back * gain_rows[1]
    dots = jnp.stack([jnp.sum(queries * query_gg, axis=1), jnp.sum(keys * key_gg, axis=1)])
    value_term = mm(normed_attn, value_low, 0, 0).astype(BF16)
    value_term, dots = lax.optimization_barrier((value_term, dots))
    value_term = lax.psum_scatter(value_term, "f", scatter_dimension=0, tiled=True)
    scales = from_position(scales, seq, chips).T
    query_scale, key_scale = scales[:, 0:1], scales[:, 1:2]
    gain1 = jnp.sum(query_back * queries * query_scale, axis=0)
    gain2 = jnp.sum(key_back * keys * key_scale, axis=0)
    dots, gain_qk = small_sum(dots, seq, chips, jnp.stack([gain1, gain2]))
    dots = from_position(dots / width, seq, chips).T
    query_pre = query_gg * query_scale - queries * (query_scale**3 * dots[:, 0:1])
    key_pre = key_gg * key_scale - keys * (key_scale**3 * dots[:, 1:2])
    pre_low = jnp.concatenate([query_pre.astype(BF16), key_pre.astype(BF16)], axis=1)
    qk_term = mm(normed_attn, pre_low, 0, 0).astype(BF16)
    qk_term = lax.psum_scatter(qk_term, "f", scatter_dimension=0, tiled=True)
    projected_grad = jnp.concatenate([pre_low, value_low], axis=1)
    back_other = mm(projected_grad[group:], qkv_part, 1, 1).astype(BF16)
    back_own = mm(projected_grad[:group], qkv_part, 1, 1)
    own, parts = seq_parts(back_own, back_other, chips)
    attn_back = own + sum(p.astype(F32) for p in parts)
    scaled = attn_back * gains[0]
    grad_tokens = res_grad + (
        scaled * in_scale - inputs * in_scale**3 * jnp.mean(inputs * scaled, axis=-1, keepdims=True)
    )

    attended_both = attended
    res_both = jnp.concatenate([res_near, res_far], axis=0)
    out_term = mm(attended_both, res_both, 0, 0).astype(BF16).reshape(planes, rows, width)
    pieces = []
    for j in range(planes):
        pairs = [
            (lanes * f + s, half * s + (f - j) % planes) for f in range(planes) for s in range(lanes)
        ]
        block = lax.dynamic_index_in_dim(out_term, (here_f - j) % planes, 0, keepdims=False)
        pieces.append(lax.ppermute(block, SEQ, pairs))
    pieces = jnp.stack(pieces)
    grad_out = plane_reduce(
        [
            lax.dynamic_index_in_dim(pieces, ((plane ^ k) - b_of) % planes, 0, keepdims=False).astype(F32)
            for k in range(planes)
        ],
        planes,
    )

    gain3 = gain3[0]
    gain_high = gain3.astype(BF16)
    gain_low = (gain3 - gain_high.astype(F32)).astype(BF16)
    extra = jnp.concatenate(
        [logit_wide, gain_high.reshape(-1, LANES), gain_low.reshape(-1, LANES)], axis=0
    )
    extras = [extra] + [swap(extra, "q", chips, k) for k in range(1, chips)]
    logit_near = jnp.concatenate([e[:count] for e in extras], axis=0)
    x_near = jnp.concatenate(x_blocks[0], axis=0)
    router_term = mm(x_near, logit_near, 0, 0)
    gain_term = sum(e[count:].astype(F32) for e in extras)
    gain_term = jnp.sum(gain_term.reshape(2, width), axis=0)
    small = jnp.concatenate(
        [router_term[:, :expert_count], gain_term[:, None]], axis=1
    ).reshape(planes, seqs, rows, expert_count + 1)
    small_own = lax.dynamic_index_in_dim(small, seq, 1, keepdims=False)
    small_other = lax.dynamic_index_in_dim(small, seq ^ 1, 1, keepdims=False)
    small_own = small_own + swap(small_other, "c", 2, 1)
    small_sum_z = lax.dynamic_index_in_dim(small_own, plane, 0, keepdims=False)
    for k in range(1, planes):
        piece = lax.dynamic_index_in_dim(small_own, plane ^ k, 0, keepdims=False)
        small_sum_z = small_sum_z + swap(piece, "f", planes, k)
    grad_router = small_sum_z[:, :expert_count]

    back_qkv = jnp.concatenate([qk_term, value_term], axis=1).reshape(seqs, rows, 3 * part)
    grad_qkv = lax.all_to_all(back_qkv, SEQ, split_axis=0, concat_axis=0, tiled=True)
    grad_qkv = (
        grad_qkv.reshape(seqs, rows, 3, part)
        .transpose(1, 2, 0, 3)
        .reshape(rows, 3 * width)
        .astype(F32)
    )
    gain_qk = gain_qk.reshape(seqs, 2, part).swapaxes(0, 1)
    gain_qk = lax.dynamic_index_in_dim(gain_qk.reshape(2, planes, seqs, rows), seq, 2, keepdims=False)
    gain_sum = lax.dynamic_index_in_dim(gain_qk, plane, 1, keepdims=False)
    for k in range(1, planes):
        piece = lax.dynamic_index_in_dim(gain_qk, plane ^ k, 1, keepdims=False)
        gain_sum = gain_sum + swap(piece, "f", planes, k)
    own_gain = lax.dynamic_slice_in_dim(gains[0], (plane * seqs + seq) * rows, rows)
    gain0 = jnp.sum(w_qkv.astype(F32) * grad_qkv, axis=1) / own_gain
    grad_gains = jnp.concatenate(
        [gain0[None], gain_sum, small_sum_z[:, expert_count][None]], axis=0
    )
    return (
        output,
        grad_tokens,
        grad_gains,
        grad_qkv,
        grad_out,
        grad_router,
        grad_gate,
        grad_up,
        grad_down,
    )


def solution(mesh):
    devices = mesh.devices
    inner = Mesh(devices.reshape(devices.shape[0], devices.shape[1] // 2, 2), ("f", "q", "c"))
    all_axes = ("f", "q", "c")
    by_rows = P(all_axes, None)
    expert = P(SEQ, "f", None)

    return jax.shard_map(
        shards,
        mesh=inner,
        in_specs=(by_rows, by_rows, P(), by_rows, by_rows, by_rows, expert, expert, expert, by_rows),
        out_specs=(
            by_rows,
            by_rows,
            P(None, all_axes),
            by_rows,
            by_rows,
            by_rows,
            expert,
            expert,
            expert,
        ),
        check_vma=False,
    )
```

```python
import functools

import jax
import jax.numpy as jnp
from jax import lax
from jax.experimental import pallas as pl
from jax.experimental.pallas import tpu as pltpu
from jax.sharding import Mesh, PartitionSpec as P


HEAD = 128
LANES = 128

BF16 = jnp.bfloat16
F32 = jnp.float32

epsilon = 1e-05
rotary_base = 10000.0

SEQ = ("q", "c")


def mm(a, b, ca, cb):
    return lax.dot_general(a, b, (((ca,), (cb,)), ((), ())), preferred_element_type=F32)


def swap(value, axis, count, k):
    return lax.ppermute(value, axis, [(i, i ^ k) for i in range(count)])


def after(value, *others):
    return lax.optimization_barrier((value, *others))[0]


def vmem_params(count):
    return pltpu.CompilerParams(
        dimension_semantics=("arbitrary",) * count, vmem_limit_bytes=60 * 1024 * 1024
    )


def held(shape, index_map):
    return pl.BlockSpec(shape, index_map, pipeline_mode=pl.Buffered(1))


def cost(flops, nbytes):
    return pl.CostEstimate(flops=int(flops), bytes_accessed=int(nbytes), transcendentals=0)


def pack_kernel(where, gate_ref, up_ref, *out_refs):
    planes = len(out_refs)
    size = gate_ref.shape[2] // planes
    for k in range(planes):
        columns = pl.ds(pl.multiple_of((where[0] ^ k) * size, 128), size)
        out_refs[k][:, :size] = gate_ref[0, :, columns]
        out_refs[k][:, size:] = up_ref[0, :, columns]


def pack_experts(where, w_gate, w_up, planes):
    experts, slab, full = w_gate.shape
    size = full // planes
    spec = pl.BlockSpec((1, slab, full), lambda e, s: (e, 0, 0))
    out = pl.BlockSpec((slab, 2 * size), lambda e, s: (0, e))
    return pl.pallas_call(
        pack_kernel,
        grid_spec=pltpu.PrefetchScalarGridSpec(
            num_scalar_prefetch=1, grid=(experts,), in_specs=[spec, spec], out_specs=[out] * planes
        ),
        out_shape=[jax.ShapeDtypeStruct((slab, 2 * experts * size), BF16)] * planes,
        compiler_params=vmem_params(1),
        name="pack",
    )(where, w_gate, w_up)


def place_kernel(where, *refs):
    out_ref = refs[-1]
    for k, piece in enumerate(refs[:-1]):
        size = piece.shape[0]
        out_ref[pl.ds(pl.multiple_of((where[0] ^ k) * size, 128), size), :] = piece[...]


def place_rows(where, pieces):
    rows, columns = pieces[0].shape
    full = rows * len(pieces)
    half = columns // 2
    return pl.pallas_call(
        place_kernel,
        grid_spec=pltpu.PrefetchScalarGridSpec(
            num_scalar_prefetch=1,
            grid=(2,),
            in_specs=[pl.BlockSpec((rows, half), lambda i, s: (0, i))] * len(pieces),
            out_specs=pl.BlockSpec((full, half), lambda i, s: (0, i)),
        ),
        out_shape=jax.ShapeDtypeStruct((full, columns), BF16),
        compiler_params=vmem_params(1),
        name="place",
    )(where, *pieces)


def unpack_kernel(where, *refs):
    gate_ref, up_ref = refs[-2:]
    size = refs[0].shape[1] // 2
    for k, piece in enumerate(refs[:-2]):
        columns = pl.ds(pl.multiple_of((where[0] ^ k) * size, 128), size)
        gate_ref[0, :, columns] = piece[:, :size].astype(F32)
        up_ref[0, :, columns] = piece[:, size:].astype(F32)


def unpack_experts(where, pieces, experts):
    slab, columns = pieces[0].shape
    size = columns // (2 * experts)
    full = size * len(pieces)
    spec = pl.BlockSpec((slab, 2 * size), lambda e, s: (0, e))
    out = pl.BlockSpec((1, slab, full), lambda e, s: (e, 0, 0))
    shape = jax.ShapeDtypeStruct((experts, slab, full), F32)
    return pl.pallas_call(
        unpack_kernel,
        grid_spec=pltpu.PrefetchScalarGridSpec(
            num_scalar_prefetch=1,
            grid=(experts,),
            in_specs=[spec] * len(pieces),
            out_specs=[out, out],
        ),
        out_shape=[shape, shape],
        compiler_params=vmem_params(1),
        name="unpack",
    )(where, *pieces)


def moe_kernel(count, experts, own_experts, aliased, where, *refs):
    x_refs, y_refs = refs[:count], refs[count : 2 * count]
    router_ref = refs[2 * count]
    gu_refs, down_refs = refs[2 * count + 1 : 2 * count + 3], refs[2 * count + 3 : 2 * count + 5]
    refs = refs[2 * count + 5 + (count if aliased else 0) :]
    dx_refs, out_refs = refs[:count], refs[count : 2 * count]
    act_ref, grad_ref = refs[2 * count : 2 * count + 2]
    xs, ys, gu_all, down_all, prob_sum, sems = refs[2 * count + 2 :]
    rows, width = x_refs[0].shape
    steps, size = down_all.shape[:2]

    for e in range(steps):
        side, i = divmod(e, own_experts)
        cols = slice(i * 2 * size, (i + 1) * 2 * size)
        lines = slice(i * size, (i + 1) * size)
        pltpu.make_async_copy(gu_refs[side].at[:, cols], gu_all.at[e], sems.at[0, e]).start()
        pltpu.make_async_copy(down_refs[side].at[lines, :], down_all.at[e], sems.at[1, e]).start()
    for i in range(count):
        here = slice(i * rows, (i + 1) * rows)
        xs[here, :] = x_refs[i][...]
        ys[here, :] = y_refs[i][:, :width]
    logits = mm(xs[...], router_ref[...], 1, 0)
    lane = lax.broadcasted_iota(jnp.int32, logits.shape, 1)
    logits = jnp.where(lane < experts, logits, -jnp.inf)
    spread = jnp.exp(logits - jnp.max(logits, axis=1, keepdims=True))
    probs = spread / jnp.sum(spread, axis=1, keepdims=True)
    weight = probs * jnp.concatenate([y[:, width:].astype(F32) for y in y_refs], axis=0)
    prob_sum[...] = jnp.zeros_like(prob_sum)

    def one_expert(e, carry):
        pltpu.make_async_copy(gu_all.at[e], gu_all.at[e], sems.at[0, e]).wait()
        pltpu.make_async_copy(down_all.at[e], down_all.at[e], sems.at[1, e]).wait()
        which = jnp.where(
            e < own_experts,
            where[1] * own_experts + e,
            (where[1] ^ 1) * own_experts + e - own_experts,
        )
        prob = jnp.sum(jnp.where(lane == which, weight, 0.0), axis=1, keepdims=True)
        both = mm(xs[...], gu_all[e], 1, 0)
        gate, up = both[:, :size], both[:, size:]
        sig = 1.0 / (1.0 + jnp.exp(-gate))
        back = mm(ys[...], down_all[e], 1, 1)
        silu = gate * sig
        act = silu * up
        prob_sum[...] += jnp.where(lane == which, jnp.sum(act * back, axis=1, keepdims=True), 0.0)
        back = back * prob
        act_ref[:, pl.ds(pl.multiple_of(e * size, size), size)] = (act * prob).astype(BF16)
        grad_ref[:, pl.ds(pl.multiple_of(2 * e * size, size), size)] = (
            back * up * sig * (1.0 + gate * (1.0 - sig))
        ).astype(BF16)
        grad_ref[:, pl.ds(pl.multiple_of((2 * e + 1) * size, size), size)] = (back * silu).astype(
            BF16
        )
        return carry

    lax.fori_loop(0, steps, one_expert, 0)
    tile = min(512, width)

    def one_tile(n, carry):
        cols = pl.ds(pl.multiple_of(n * tile, tile), tile)
        dx = out = None
        for e in range(steps):
            term = mm(grad_ref[:, 2 * e * size : 2 * (e + 1) * size], gu_all[e, cols, :], 1, 1)
            dx = term if dx is None else dx + term
            term = mm(act_ref[:, e * size : (e + 1) * size], down_all[e, :, cols], 1, 0)
            out = term if out is None else out + term
        for i in range(count):
            here = slice(i * rows, (i + 1) * rows)
            dx_refs[i][:, cols] = dx[here].astype(BF16)
            out_refs[i][:, cols] = out[here].astype(BF16)
        return carry

    lax.fori_loop(0, width // tile, one_tile, 0)
    for i in range(count):
        dx_refs[i][:, width:] = prob_sum[i * rows : (i + 1) * rows].astype(BF16)


def moe_rows(where, group, groups, xs, ys, router, gus, downs, outs, experts, own_experts):
    count = len(xs)
    rows, width = xs[0].shape
    size = downs[0].shape[0] // own_experts
    total = count * rows
    steps = 2 * own_experts
    lanes = router.shape[1]
    aliased = outs is not None

    def fixed(block):
        return lambda i, s: (block, 0)

    anywhere = pl.BlockSpec(memory_space=pl.ANY)
    in_specs = (
        [held((rows, width), fixed(0)) for _ in xs]
        + [held((rows, y.shape[1]), fixed(i)) for y, i in ys]
        + [held(router.shape, fixed(0))]
        + [anywhere] * 4
        + ([anywhere] * count if aliased else [])
    )
    out_specs = (
        [held((rows, width + lanes), fixed(0))] * count
        + [held((rows, width), fixed(group))] * count
        + [held((total, steps * size), fixed(0)), held((total, 2 * steps * size), fixed(0))]
    )
    first = 1 + 2 * count + 5
    return pl.pallas_call(
        functools.partial(moe_kernel, count, experts, own_experts, aliased),
        grid_spec=pltpu.PrefetchScalarGridSpec(
            num_scalar_prefetch=1,
            grid=(1,),
            in_specs=in_specs,
            out_specs=out_specs,
            scratch_shapes=[
                pltpu.VMEM((total, width), BF16),
                pltpu.VMEM((total, width), BF16),
                pltpu.VMEM((steps, width, 2 * size), BF16),
                pltpu.VMEM((steps, size, width), BF16),
                pltpu.VMEM((total, lanes), F32),
                pltpu.SemaphoreType.DMA((2, steps)),
            ],
        ),
        out_shape=[jax.ShapeDtypeStruct((rows, width + lanes), BF16)] * count
        + [jax.ShapeDtypeStruct((groups * rows, width), BF16)] * count
        + [
            jax.ShapeDtypeStruct((total, steps * size), BF16),
            jax.ShapeDtypeStruct((total, 2 * steps * size), BF16),
        ],
        input_output_aliases={first + i: count + i for i in range(count)} if aliased else {},
        compiler_params=vmem_params(1),
        cost_estimate=cost(
            12 * total * width * size * steps, 8 * total * width + 6 * width * size * steps
        ),
        name="moe",
    )(where, *xs, *[y for y, _ in ys], router, *gus, *downs, *(outs or []))


def norm_ffn_kernel(token_ref, own_ref, *refs):
    gain_ref, res_ref, low_ref = refs[-3:]
    total = token_ref[...].astype(F32) + own_ref[...]
    for ref in refs[:-3]:
        total = total + ref[...].astype(F32)
    res_ref[...] = total
    scale = lax.rsqrt(jnp.mean(total * total, axis=1, keepdims=True) + epsilon)
    low_ref[...] = (total * scale * gain_ref[...]).astype(BF16)


def norm_ffn(tokens, own, parts, gain):
    return pl.pallas_call(
        norm_ffn_kernel,
        out_shape=[
            jax.ShapeDtypeStruct(tokens.shape, F32),
            jax.ShapeDtypeStruct(tokens.shape, BF16),
        ],
        compiler_params=vmem_params(0),
        cost_estimate=cost(10 * tokens.size, 16 * tokens.size),
        name="nffn",
    )(tokens, own, *parts, gain)


def norm_back_kernel(experts, low_ref, res_ref, router_ref, wide_ref, gain_ref, *refs):
    grad_ref, grad_low_ref, logit_ref, gain_out = refs[-4:]
    width = res_ref.shape[1]
    total = refs[0][...].astype(F32)
    for ref in refs[1:-4]:
        total = total + ref[...].astype(F32)
    upstream = wide_ref[:, :width].astype(F32)
    mask = wide_ref[:, width:].astype(F32)
    logits = mm(low_ref[...], router_ref[...], 1, 0)
    lane = lax.broadcasted_iota(jnp.int32, logits.shape, 1)
    logits = jnp.where(lane < experts, logits, -jnp.inf)
    spread = jnp.exp(logits - jnp.max(logits, axis=1, keepdims=True))
    probs = spread / jnp.sum(spread, axis=1, keepdims=True)
    prob_full = total[:, width:] * mask
    logit = (
        probs * (prob_full - jnp.sum(probs * prob_full, axis=1, keepdims=True))
    ).astype(BF16)
    logit_ref[...] = logit
    dn = total[:, :width] + mm(logit, router_ref[...], 1, 1)
    residual = res_ref[...]
    scale = lax.rsqrt(jnp.mean(residual * residual, axis=1, keepdims=True) + epsilon)
    scaled = dn * gain_ref[...]
    grad = upstream + (
        scaled * scale - residual * (scale**3 * jnp.mean(residual * scaled, axis=1, keepdims=True))
    )
    grad_ref[...] = grad
    grad_low_ref[...] = grad.astype(BF16)
    gain_out[...] = jnp.sum(dn * residual * scale, axis=0, keepdims=True)


def norm_back(low, residual, router, wide, gain, parts, experts):
    count, width = residual.shape
    return pl.pallas_call(
        functools.partial(norm_back_kernel, experts),
        out_shape=[
            jax.ShapeDtypeStruct((count, width), F32),
            jax.ShapeDtypeStruct((count, width), BF16),
            jax.ShapeDtypeStruct((count, router.shape[1]), BF16),
            jax.ShapeDtypeStruct((1, width), F32),
        ],
        compiler_params=vmem_params(0),
        cost_estimate=cost(20 * low.size, 30 * low.size),
        name="nback",
    )(low, residual, router, wide, gain, *parts)


def merge_kernel(planes, where, own_ref, other_ref, *out_refs):
    total = own_ref[...].astype(F32) + other_ref[...].astype(F32)
    k = pl.program_id(0)
    for i in range(planes):

        @pl.when(k == i)
        def _(i=i):
            out_refs[i][...] = total.astype(BF16)


def merge_parts(where, own, other, planes):
    slab, columns = own.shape[0] // planes, own.shape[1]
    spec = pl.BlockSpec((slab, columns), lambda k, s: (s[0] ^ k, 0))
    return pl.pallas_call(
        functools.partial(merge_kernel, planes),
        grid_spec=pltpu.PrefetchScalarGridSpec(
            num_scalar_prefetch=1,
            grid=(planes,),
            in_specs=[spec, spec],
            out_specs=[pl.BlockSpec((slab, columns), lambda k, s: (0, 0))] * planes,
        ),
        out_shape=[jax.ShapeDtypeStruct((slab, columns), BF16)] * planes,
        compiler_params=vmem_params(1),
        cost_estimate=cost(own.size, 6 * own.size),
        name="merge",
    )(where, own, other)


def grad_in_kernel(groups, count, where, *refs):
    x_refs = refs[: groups * count]
    g_refs = refs[groups * count : groups * count + groups]
    own_ref, other_ref, xs = refs[groups * count + groups :]
    rows = x_refs[0].shape[0]
    half = own_ref.shape[1]
    for i, x in enumerate(x_refs):
        xs[i * rows : (i + 1) * rows, :] = x[...]
    step = count * rows
    for out, start in ((own_ref, 0), (other_ref, half)):
        total = None
        for g in range(groups):
            term = mm(
                xs[g * step : (g + 1) * step, :], g_refs[g][:, start : start + half], 0, 0
            )
            total = term if total is None else total + term
        out[...] = total.astype(BF16)


def grad_in(where, xs, grads, tile=256):
    groups, count = len(grads), len(xs) // len(grads)
    rows, width = xs[0].shape
    columns = grads[0].shape[1]
    shape = jax.ShapeDtypeStruct((width, columns // 2), BF16)
    return pl.pallas_call(
        functools.partial(grad_in_kernel, groups, count),
        grid_spec=pltpu.PrefetchScalarGridSpec(
            num_scalar_prefetch=1,
            grid=(width // tile,),
            in_specs=[pl.BlockSpec((rows, tile), lambda i, s: (0, i))] * len(xs)
            + [held(g.shape, lambda i, s: (0, 0)) for g in grads],
            out_specs=[pl.BlockSpec((tile, columns // 2), lambda i, s: (i, 0))] * 2,
            scratch_shapes=[pltpu.VMEM((rows * len(xs), tile), BF16)],
        ),
        out_shape=[shape, shape],
        compiler_params=vmem_params(1),
        cost_estimate=cost(
            2 * rows * len(xs) * width * columns, 2 * rows * len(xs) * (width + columns)
        ),
        name="gin",
    )(where, *xs, *grads)


def grad_down_kernel(places, own_steps, where, *refs):
    y_refs = refs[: len(places)]
    groups = len(refs) - len(places) - 3
    a_refs = refs[len(places) : len(places) + groups]
    own_ref, other_ref, ys = refs[len(places) + groups :]
    e = pl.program_id(1)

    @pl.when(e == 0)
    def _():
        for ref, there in zip(y_refs, places):
            size = ref.shape[0] // len(there)
            for i, place in enumerate(there):
                ys[place * size : (place + 1) * size, :] = ref[i * size : (i + 1) * size, :]

    step = a_refs[0].shape[0]
    total = None
    for g in range(groups):
        term = mm(a_refs[g][...], ys[g * step : (g + 1) * step, :], 0, 0)
        total = term if total is None else total + term

    @pl.when(e < own_steps)
    def _():
        own_ref[...] = total

    @pl.when(e >= own_steps)
    def _():
        other_ref[...] = total.astype(BF16)


def grad_down_rows(where, ys, places, acts, width, own_experts):
    size = acts[0].shape[1] // (2 * own_experts)
    last = own_experts - 1
    total = acts[0].shape[0] * len(acts)
    tile = width
    while total * tile > 1 << 21:
        tile //= 2
    return pl.pallas_call(
        functools.partial(grad_down_kernel, places, own_experts),
        grid_spec=pltpu.PrefetchScalarGridSpec(
            num_scalar_prefetch=1,
            grid=(width // tile, 2 * own_experts),
            in_specs=[pl.BlockSpec((y.shape[0], tile), lambda j, e, s: (0, j)) for y in ys]
            + [pl.BlockSpec((a.shape[0], size), lambda j, e, s: (0, e)) for a in acts],
            out_specs=[
                pl.BlockSpec((size, tile), lambda j, e, s: (jnp.minimum(e, last), j)),
                pl.BlockSpec((size, tile), lambda j, e, s: (jnp.maximum(e - own_experts, 0), j)),
            ],
            scratch_shapes=[pltpu.VMEM((total, tile), BF16)],
        ),
        out_shape=[
            jax.ShapeDtypeStruct((own_experts * size, width), F32),
            jax.ShapeDtypeStruct((own_experts * size, width), BF16),
        ],
        compiler_params=vmem_params(2),
        cost_estimate=cost(
            4 * total * width * size * own_experts, 2 * total * (width + 2 * size * own_experts)
        ),
        name="gdown",
    )(where, *ys, *acts)


def block_rows(seq, block, seqs, size):
    k = seq ^ block
    return pl.ds(pl.multiple_of(((k & 1) * (seqs // 2) + (k >> 1)) * size, size), size)


def turned(values, cosine, sine):
    return values * cosine + pltpu.roll(values, values.shape[1] // 2, 1) * sine


def attend_kernel(seqs, tile, where, q_ref, k_ref, v_ref, scale_ref, gain_ref, cos_ref, sin_ref, att_ref, ql, kl, vl, lse_ref):
    length, head = q_ref.shape
    size = length // seqs
    for b in range(seqs):
        rows = block_rows(where[1], b, seqs, size)
        here = slice(b * size, (b + 1) * size)
        cosine, sine = cos_ref[here, :], sin_ref[here, :]
        scales = scale_ref[here, :]
        ql[here, :] = turned(
            q_ref[rows, :] * scales[:, 0:1] * gain_ref[0:1, :], cosine, sine
        ).astype(BF16)
        kl[here, :] = turned(
            k_ref[rows, :] * scales[:, 1:2] * gain_ref[1:2, :], cosine, sine
        ).astype(BF16)
        vl[here, :] = v_ref[rows, :].astype(BF16)
    diagonal = lax.broadcasted_iota(jnp.int32, (tile, tile), 0) >= lax.broadcasted_iota(
        jnp.int32, (tile, tile), 1
    )
    for t in range(length // tile):
        here = slice(t * tile, (t + 1) * tile)
        limit = (t + 1) * tile
        scores = mm(ql[here, :], kl[:limit, :], 1, 1) * (head ** (-0.5))
        edge = jnp.where(diagonal, scores[:, t * tile :], -jnp.inf)
        scores = jnp.concatenate([scores[:, : t * tile], edge], axis=1) if t else edge
        peak = jnp.max(scores, axis=1, keepdims=True)
        spread = jnp.exp(scores - peak)
        total = jnp.sum(spread, axis=1, keepdims=True)
        weights = (spread * (1.0 / total)).astype(BF16)
        out = mm(weights, vl[:limit, :], 1, 0).astype(BF16)
        lse_ref[here, :] = jnp.broadcast_to(peak + jnp.log(total), (tile, head))
        for b in range(tile // size):
            rows = block_rows(where[1], t * (tile // size) + b, seqs, size)
            att_ref[rows, :] = out[b * size : (b + 1) * size]


def attend(where, projected, scales, gain_rows, cosine, sine, seqs, heads, tile=256):
    length = projected.shape[0]
    head = projected.shape[1] // (3 * heads)
    part = heads * head

    def column(offset):
        return pl.BlockSpec((length, head), lambda h, s: (0, offset + h))

    full = pl.BlockSpec((length, head), lambda h, s: (0, 0))
    low = jax.ShapeDtypeStruct((length, part), BF16)
    return pl.pallas_call(
        functools.partial(attend_kernel, seqs, tile),
        grid_spec=pltpu.PrefetchScalarGridSpec(
            num_scalar_prefetch=1,
            grid=(heads,),
            in_specs=[
                column(0),
                column(heads),
                column(2 * heads),
                pl.BlockSpec(scales.shape, lambda h, s: (0, 0)),
                pl.BlockSpec((2, head), lambda h, s: (0, h)),
                full,
                full,
            ],
            out_specs=[column(0)] * 5,
        ),
        out_shape=[low, low, low, low, jax.ShapeDtypeStruct((length, part), F32)],
        compiler_params=vmem_params(1),
        cost_estimate=cost(4 * length * length * part, 20 * length * part),
        name="att",
    )(where, projected, projected, projected, scales, gain_rows, cosine, sine)


def attend_back_kernel(seqs, tile, where, q_ref, k_ref, v_ref, lse_ref, grad_ref, cos_ref, sin_ref, dq_ref, dk_ref, dv_ref, go, dk, dv):
    length, head = q_ref.shape
    size = length // seqs
    scale = head ** (-0.5)
    for b in range(seqs):
        go[b * size : (b + 1) * size, :] = grad_ref[block_rows(where[1], b, seqs, size), :]
    dk[...] = jnp.zeros_like(dk)
    dv[...] = jnp.zeros_like(dv)
    diagonal = lax.broadcasted_iota(jnp.int32, (tile, tile), 0) >= lax.broadcasted_iota(
        jnp.int32, (tile, tile), 1
    )
    for t in range(length // tile):
        here = slice(t * tile, (t + 1) * tile)
        limit = (t + 1) * tile
        scores = mm(q_ref[here, :], k_ref[:limit, :], 1, 1) * scale
        edge = jnp.where(diagonal, scores[:, t * tile :], -jnp.inf)
        scores = jnp.concatenate([scores[:, : t * tile], edge], axis=1) if t else edge
        probs = jnp.exp(scores - lse_ref[here, 0:1])
        dprobs = mm(go[here, :], v_ref[:limit, :], 1, 1)
        terms = probs * dprobs
        dscores = (terms - probs * jnp.sum(terms, axis=1, keepdims=True)).astype(BF16)
        dq = (mm(dscores, k_ref[:limit, :], 1, 0) * scale).astype(BF16).astype(F32)
        dq = turned(dq, cos_ref[here, :], -sin_ref[here, :])
        for b in range(tile // size):
            rows = block_rows(where[1], t * (tile // size) + b, seqs, size)
            dq_ref[rows, :] = dq[b * size : (b + 1) * size]
        dk[:limit, :] += mm(dscores, q_ref[here, :], 0, 0)
        dv[:limit, :] += mm(probs.astype(BF16), go[here, :], 0, 0)
    for b in range(seqs):
        here = slice(b * size, (b + 1) * size)
        rows = block_rows(where[1], b, seqs, size)
        back = (dk[here, :] * scale).astype(BF16).astype(F32)
        dk_ref[rows, :] = turned(back, cos_ref[here, :], -sin_ref[here, :])
        dv_ref[rows, :] = dv[here, :].astype(BF16)


def attend_back(where, ql, kl, vl, lse, grads, cosine, sine, seqs, heads, tile=256):
    length, part = ql.shape
    head = part // heads
    column = pl.BlockSpec((length, head), lambda h, s: (0, h))
    full = pl.BlockSpec((length, head), lambda h, s: (0, 0))
    wide = jax.ShapeDtypeStruct((length, part), F32)
    return pl.pallas_call(
        functools.partial(attend_back_kernel, seqs, tile),
        grid_spec=pltpu.PrefetchScalarGridSpec(
            num_scalar_prefetch=1,
            grid=(heads,),
            in_specs=[column] * 5 + [full, full],
            out_specs=[column] * 3,
            scratch_shapes=[
                pltpu.VMEM((length, head), BF16),
                pltpu.VMEM((length, head), F32),
                pltpu.VMEM((length, head), F32),
            ],
        ),
        out_shape=[wide, wide, jax.ShapeDtypeStruct((length, part), BF16)],
        compiler_params=vmem_params(1),
        cost_estimate=cost(10 * length * length * part, 24 * length * part),
        name="aback",
    )(where, ql, kl, vl, lse, grads, cosine, sine)


def seq_gather(block, chips):
    near = [block] + [swap(block, "q", chips, k) for k in range(1, chips)]
    near = jnp.concatenate(near, axis=0)
    return near, swap(near, "c", 2, 1)


def seq_parts(own, other, chips):
    total = own + swap(other, "c", 2, 1).astype(F32)
    rows = total.shape[0] // chips
    low = total[rows:].astype(BF16)
    parts = [swap(low[(k - 1) * rows : k * rows], "q", chips, k) for k in range(1, chips)]
    return total[:rows], parts


def masks_of(planes):
    return [3, 1] if planes == 4 else [1 << i for i in range(planes.bit_length() - 1)]


def plane_gather(block, planes):
    rows = block.shape[0]
    have, parts = {0: (block, 0)}, [(block, [0])]
    for mask in masks_of(planes):
        keys = [k for _, ks in parts for k in ks]
        sent = parts[0][0] if len(parts) == 1 else jnp.concatenate([a for a, _ in parts], axis=0)
        arrived = swap(sent, "f", planes, mask)
        keys = [k ^ mask for k in keys]
        parts.append((arrived, keys))
        have.update({k: (arrived, j) for j, k in enumerate(keys)})
    return have, parts[1:], rows


def plane_reduce(blocks, planes):
    held_back = dict(enumerate(blocks))
    for i, mask in enumerate(reversed(masks_of(planes))):
        span = {0}
        for other in masks_of(planes)[: len(masks_of(planes)) - 1 - i]:
            span |= {k ^ other for k in span}
        keys = sorted(span)
        sent = jnp.concatenate([held_back[k ^ mask].astype(BF16) for k in keys], axis=0)
        rows = sent.shape[0] // len(keys)
        arrived = swap(sent, "f", planes, mask)
        held_back = {
            k: held_back[k] + arrived[j * rows : (j + 1) * rows].astype(F32)
            for j, k in enumerate(keys)
        }
    return held_back[0]


def by_bits(values, index, axis):
    size = values.shape[axis]
    bit = 1
    while bit < size:
        pieces = [lax.slice_in_dim(values, i, i + bit, axis=axis) for i in range(0, size, bit)]
        turned_over = jnp.concatenate([pieces[i ^ 1] for i in range(len(pieces))], axis=axis)
        values = jnp.where((index & bit) > 0, turned_over, values)
        bit *= 2
    return values


def to_position(values, seq, chips):
    n = values.shape[0]
    values = values.reshape(n, 2, chips, -1)
    values = by_bits(by_bits(values, seq & 1, 1), seq >> 1, 2)
    return values.swapaxes(1, 2).reshape(n, -1)


def from_position(values, seq, chips):
    n = values.shape[0]
    values = values.reshape(n, chips, 2, -1).swapaxes(1, 2)
    return by_bits(by_bits(values, seq & 1, 1), seq >> 1, 2).reshape(n, -1)


def small_sum(pair, seq, chips, rider=None):
    flat = to_position(pair, seq, chips).reshape(-1, LANES)
    count = flat.shape[0]
    if rider is not None:
        flat = jnp.concatenate([flat, rider.reshape(-1, LANES)], axis=0)
    every = lax.all_gather(flat, SEQ, axis=0)
    total = jnp.sum(every[:, :count], axis=0).reshape(pair.shape)
    return total if rider is None else (total, every[:, count:])


def shards(tokens, cotangent, gains, w_qkv, w_out, w_router, w_gate, w_up, w_down, routes):
    planes = lax.axis_size("f")
    chips = lax.axis_size("q")
    seqs = 2 * chips
    plane = lax.axis_index("f")
    seq = 2 * lax.axis_index("q") + lax.axis_index("c")
    where = jnp.stack([plane, seq]).astype(jnp.int32)
    count, width = tokens.shape
    length = count * seqs
    part = width // seqs
    heads = part // HEAD
    rows = w_qkv.shape[0]
    expert_count = w_router.shape[1]
    own_experts, _ = w_gate.shape[:2]
    slice_ff = w_down.shape[1]
    cut = own_experts * slice_ff

    columns = w_qkv.reshape(rows, 3, seqs, part).transpose(2, 0, 1, 3).reshape(seqs, rows, 3 * part)
    router_wide = jnp.pad(w_router, ((0, 0), (0, LANES - expert_count)))
    columns = jnp.concatenate(
        [columns, jnp.broadcast_to(router_wide, (seqs, rows, LANES))], axis=2
    )
    columns = lax.all_to_all(columns, SEQ, split_axis=0, concat_axis=0, tiled=True)

    mask = jnp.sum(
        (routes[:, :, None] == jnp.arange(expert_count, dtype=jnp.int32)[None, None, :]).astype(F32),
        axis=1,
    )
    wide = jnp.concatenate(
        [cotangent, jnp.pad(mask, ((0, 0), (0, LANES - expert_count))).astype(BF16)], axis=1
    )
    _, dy_parts, _ = plane_gather(wide, planes)

    inputs = tokens.astype(F32)
    in_scale = lax.rsqrt(jnp.mean(inputs * inputs, axis=-1, keepdims=True) + epsilon)
    normed_own = (inputs * in_scale * gains[0]).astype(BF16)
    near, far = seq_gather(after(normed_own, columns), chips)
    normed_attn = jnp.concatenate([near, far], axis=0)
    dy_far = []
    for value, there in dy_parts:
        dy_far.append(([value] + [swap(value, "q", chips, k) for k in range(1, chips)], there))
    dy_near = [wide] + [swap(wide, "q", chips, k) for k in range(1, chips)]

    columns = columns.reshape(seqs * rows, 3 * part + LANES)
    router_own = columns[:, 3 * part :]
    columns = after(columns[:, : 3 * part], dy_parts[-1][0])
    qkv_part = lax.all_gather(columns, "f", axis=0, tiled=True)
    nearest = sorted(range(1, planes), key=lambda k: -k if planes == 4 and k == 3 else k)
    out_z, router = {0: w_out}, {0: router_own}
    for k in nearest:
        out_z[k] = swap(w_out, "f", planes, k)
    for k in nearest:
        router[k] = swap(router_own, "f", planes, k)
    out_z = jnp.stack([out_z[k] for k in range(planes)])
    router = jnp.stack([router[k] for k in range(planes)])
    router = by_bits(router, plane, 0).reshape(width, LANES)

    half = seqs // 2
    lanes = seqs // planes
    b_of = seq % half
    here_f = seq // lanes
    blocks = []
    for j in range(planes):
        pairs = [
            (half * s + (f - j) % planes, lanes * f + s) for f in range(planes) for s in range(lanes)
        ]
        block = lax.dynamic_index_in_dim(
            out_z, ((b_of + j) % planes) ^ plane, 0, keepdims=False
        )
        blocks.append(lax.ppermute(block, SEQ, pairs))
    order = (here_f - jnp.arange(planes)) % planes
    out_rows = jnp.take(jnp.stack(blocks), order, axis=0).reshape(part, width)

    packed = pack_experts(where, w_gate, w_up, planes)
    qkv_part, *packed = lax.optimization_barrier((qkv_part, *packed))
    arrived = [packed[0]]
    for k in range(1, planes):
        arrived.append(swap(packed[k], "f", planes, k))
    own_gu = place_rows(where, arrived)
    other_gu = swap(own_gu, "c", 2, 1)
    own_down = w_down.reshape(cut, width)
    other_down = swap(own_down, "c", 2, 1)

    exponent_index = jnp.arange(HEAD // 2, dtype=F32) * (2.0 / HEAD)
    angles = jnp.arange(length, dtype=F32)[:, None] * (rotary_base ** (-exponent_index))[None, :]
    cosine, sine = jnp.cos(angles), jnp.sin(angles)
    cosine = jnp.concatenate([cosine, cosine], axis=1)
    sine = jnp.concatenate([-sine, sine], axis=1)
    cosine, sine = lax.optimization_barrier((cosine, sine))

    projected = mm(normed_attn, qkv_part, 1, 0)
    queries, keys = projected[:, :part], projected[:, part : 2 * part]
    squares = jnp.stack([jnp.sum(queries * queries, axis=1), jnp.sum(keys * keys, axis=1)])
    scales = lax.rsqrt(small_sum(squares, seq, chips) / width + epsilon)
    gain_rows = lax.dynamic_slice_in_dim(gains[1:3], seq * part, part, axis=1)
    attended, ql, kl, vl, lse = attend(
        where, projected, scales.T, gain_rows, cosine, sine, seqs, heads
    )
    group = chips * count
    out_other = mm(attended[group:], out_rows, 1, 0).astype(BF16)
    out_own = mm(attended[:group], out_rows, 1, 0)
    own, parts = seq_parts(out_own, out_other, chips)
    gain_ffn = gains[3:4]
    residual, normed_low = norm_ffn(tokens, own, parts, gain_ffn)

    x_blocks, x_planes = [], {}
    for f in range(planes):
        block = normed_low
        if planes == 4 and f == 2:
            block = swap(x_planes[3], "f", planes, 1)
        elif f:
            block = x_planes[f] if f in x_planes else swap(normed_low, "f", planes, f)
        if planes == 4 and f == 1:
            x_planes[3] = swap(normed_low, "f", planes, 3)
        x_blocks.append([block] + [swap(block, "q", chips, k) for k in range(1, chips)])

    acts, grads, outs, back_parts = [], [], None, []
    tight = planes * chips > 16
    for f in range(planes):
        if tight and f > 1:
            x_blocks[f][0] = after(x_blocks[f][0], back_parts[-1])
        if f == 0:
            ys = [(y, 0) for y in dy_near]
        else:
            ys = [(y, there.index(f)) for some, there in dy_far if f in there for y in some]
        results = moe_rows(
            where,
            f,
            planes,
            x_blocks[f],
            ys,
            router,
            [own_gu, other_gu],
            [own_down, other_down],
            outs,
            expert_count,
            own_experts,
        )
        dxs, outs = results[:chips], results[chips : 2 * chips]
        acts.append(results[2 * chips])
        grads.append(results[2 * chips + 1])
        arrivals = [dxs[0]] + [swap(dxs[k], "q", chips, k) for k in range(1, chips)]
        if f:
            if planes == 4 and f == 3:
                arrivals.append(from_next)
            total = sum(a.astype(F32) for a in arrivals).astype(BF16)
            mask = 1 if planes == 4 and f == 2 else f
            arrivals = [swap(total, "f", planes, mask)]
            if planes == 4 and f == 2:
                from_next, arrivals = arrivals[0], []
        back_parts += arrivals

    groups = max(planes // 2, 1)
    block = groups * count
    total = residual
    for g in reversed(range(planes // groups)):
        pieces = []
        for k in reversed(range(1, chips)):
            pieces.append(swap(outs[k][g * block : (g + 1) * block], "q", chips, k))
        moe = after(outs[0][g * block : (g + 1) * block], *pieces).astype(F32)
        moe = moe + sum(piece.astype(F32) for piece in pieces)
        pieces = [moe[i * count : (i + 1) * count] for i in range(groups)]
        if planes == 4 and g:
            arrived = swap(pieces[0].astype(BF16), "f", planes, 1).astype(F32)
            total = total + swap((pieces[1] + arrived).astype(BF16), "f", planes, 3).astype(F32)
            continue
        for k, piece in enumerate(pieces, g * groups):
            if k:
                piece = swap(piece.astype(BF16), "f", planes, k).astype(F32)
            total = total + piece
    output = total.astype(BF16)

    x_flat = [block for group_blocks in x_blocks for block in group_blocks]
    own_part, other_part = grad_in(where, x_flat, grads)
    other_part = swap(other_part, "c", 2, 1)
    back = list(merge_parts(where, own_part, other_part, planes))
    for k in range(1, planes):
        back[k] = swap(back[k], "f", planes, k)
    grad_gate, grad_up = unpack_experts(where, back, own_experts)
    places = [[k] for k in range(chips)]
    dy_all = list(dy_near)
    for dy_some, there in dy_far:
        dy_all += dy_some
        places += [[f * chips + k for f in there] for k in range(chips)]
    down_own, down_other = grad_down_rows(where, dy_all, places, acts, width, own_experts)
    down_other = swap(down_other, "c", 2, 1)
    grad_down = (down_own + down_other.astype(F32)).reshape(own_experts, slice_ff, width)

    if tight:
        back_parts[0] = after(back_parts[0], output, down_other, *back)

    res_grad, res_low, logit_wide, gain3 = norm_back(
        normed_low, residual, router, wide, gain_ffn, back_parts, expert_count
    )

    res_near, res_far = seq_gather(res_low, chips)
    attended_grad = jnp.concatenate(
        [mm(res_near, out_rows, 1, 1), mm(res_far, out_rows, 1, 1)], axis=0
    ).astype(BF16)
    query_back, key_back, value_low = attend_back(
        where, ql, kl, vl, lse, attended_grad, cosine, sine, seqs, heads
    )
    query_gg, key_gg = query_back * gain_rows[0], key_back * gain_rows[1]
    dots = jnp.stack([jnp.sum(queries * query_gg, axis=1), jnp.sum(keys * key_gg, axis=1)])
    value_term = mm(normed_attn, value_low, 0, 0).astype(BF16)
    value_term, dots = lax.optimization_barrier((value_term, dots))
    value_term = lax.psum_scatter(value_term, "f", scatter_dimension=0, tiled=True)
    scales = from_position(scales, seq, chips).T
    query_scale, key_scale = scales[:, 0:1], scales[:, 1:2]
    gain1 = jnp.sum(query_back * queries * query_scale, axis=0)
    gain2 = jnp.sum(key_back * keys * key_scale, axis=0)
    dots, gain_qk = small_sum(dots, seq, chips, jnp.stack([gain1, gain2]))
    dots = from_position(dots / width, seq, chips).T
    query_pre = query_gg * query_scale - queries * (query_scale**3 * dots[:, 0:1])
    key_pre = key_gg * key_scale - keys * (key_scale**3 * dots[:, 1:2])
    pre_low = jnp.concatenate([query_pre.astype(BF16), key_pre.astype(BF16)], axis=1)
    qk_term = mm(normed_attn, pre_low, 0, 0).astype(BF16)
    qk_term = lax.psum_scatter(qk_term, "f", scatter_dimension=0, tiled=True)
    projected_grad = jnp.concatenate([pre_low, value_low], axis=1)
    back_other = mm(projected_grad[group:], qkv_part, 1, 1).astype(BF16)
    back_own = mm(projected_grad[:group], qkv_part, 1, 1)
    own, parts = seq_parts(back_own, back_other, chips)
    attn_back = own + sum(p.astype(F32) for p in parts)
    scaled = attn_back * gains[0]
    grad_tokens = res_grad + (
        scaled * in_scale - inputs * in_scale**3 * jnp.mean(inputs * scaled, axis=-1, keepdims=True)
    )

    attended_both = attended
    res_both = jnp.concatenate([res_near, res_far], axis=0)
    out_term = mm(attended_both, res_both, 0, 0).astype(BF16).reshape(planes, rows, width)
    pieces = []
    for j in range(planes):
        pairs = [
            (lanes * f + s, half * s + (f - j) % planes) for f in range(planes) for s in range(lanes)
        ]
        block = lax.dynamic_index_in_dim(out_term, (here_f - j) % planes, 0, keepdims=False)
        pieces.append(lax.ppermute(block, SEQ, pairs))
    pieces = jnp.stack(pieces)
    grad_out = plane_reduce(
        [
            lax.dynamic_index_in_dim(pieces, ((plane ^ k) - b_of) % planes, 0, keepdims=False).astype(F32)
            for k in range(planes)
        ],
        planes,
    )

    gain3 = gain3[0]
    gain_high = gain3.astype(BF16)
    gain_low = (gain3 - gain_high.astype(F32)).astype(BF16)
    extra = jnp.concatenate(
        [logit_wide, gain_high.reshape(-1, LANES), gain_low.reshape(-1, LANES)], axis=0
    )
    extras = [extra] + [swap(extra, "q", chips, k) for k in range(1, chips)]
    logit_near = jnp.concatenate([e[:count] for e in extras], axis=0)
    x_near = jnp.concatenate(x_blocks[0], axis=0)
    router_term = mm(x_near, logit_near, 0, 0)
    gain_term = sum(e[count:].astype(F32) for e in extras)
    gain_term = jnp.sum(gain_term.reshape(2, width), axis=0)
    small = jnp.concatenate(
        [router_term[:, :expert_count], gain_term[:, None]], axis=1
    ).reshape(planes, seqs, rows, expert_count + 1)
    small_own = lax.dynamic_index_in_dim(small, seq, 1, keepdims=False)
    small_other = lax.dynamic_index_in_dim(small, seq ^ 1, 1, keepdims=False)
    small_own = small_own + swap(small_other, "c", 2, 1)
    small_sum_z = lax.dynamic_index_in_dim(small_own, plane, 0, keepdims=False)
    for k in range(1, planes):
        piece = lax.dynamic_index_in_dim(small_own, plane ^ k, 0, keepdims=False)
        small_sum_z = small_sum_z + swap(piece, "f", planes, k)
    grad_router = small_sum_z[:, :expert_count]

    back_qkv = jnp.concatenate([qk_term, value_term], axis=1).reshape(seqs, rows, 3 * part)
    grad_qkv = lax.all_to_all(back_qkv, SEQ, split_axis=0, concat_axis=0, tiled=True)
    grad_qkv = (
        grad_qkv.reshape(seqs, rows, 3, part)
        .transpose(1, 2, 0, 3)
        .reshape(rows, 3 * width)
        .astype(F32)
    )
    gain_qk = gain_qk.reshape(seqs, 2, part).swapaxes(0, 1)
    gain_qk = lax.dynamic_index_in_dim(gain_qk.reshape(2, planes, seqs, rows), seq, 2, keepdims=False)
    gain_sum = lax.dynamic_index_in_dim(gain_qk, plane, 1, keepdims=False)
    for k in range(1, planes):
        piece = lax.dynamic_index_in_dim(gain_qk, plane ^ k, 1, keepdims=False)
        gain_sum = gain_sum + swap(piece, "f", planes, k)
    own_gain = lax.dynamic_slice_in_dim(gains[0], (plane * seqs + seq) * rows, rows)
    gain0 = jnp.sum(w_qkv.astype(F32) * grad_qkv, axis=1) / own_gain
    grad_gains = jnp.concatenate(
        [gain0[None], gain_sum, small_sum_z[:, expert_count][None]], axis=0
    )
    return (
        output,
        grad_tokens,
        grad_gains,
        grad_qkv,
        grad_out,
        grad_router,
        grad_gate,
        grad_up,
        grad_down,
    )


def solution(mesh):
    devices = mesh.devices
    inner = Mesh(devices.reshape(devices.shape[0], devices.shape[1] // 2, 2), ("f", "q", "c"))
    all_axes = ("f", "q", "c")
    by_rows = P(all_axes, None)
    expert = P(SEQ, "f", None)

    return jax.shard_map(
        shards,
        mesh=inner,
        in_specs=(by_rows, by_rows, P(), by_rows, by_rows, by_rows, expert, expert, expert, by_rows),
        out_specs=(
            by_rows,
            by_rows,
            P(None, all_axes),
            by_rows,
            by_rows,
            by_rows,
            expert,
            expert,
            expert,
        ),
        check_vma=False,
    )
```

```python
import functools

import jax
import jax.numpy as jnp
from jax import lax
from jax.experimental import pallas as pl
from jax.experimental.pallas import tpu as pltpu
from jax.sharding import Mesh, PartitionSpec as P


HEAD = 128
LANES = 128

BF16 = jnp.bfloat16
F32 = jnp.float32

epsilon = 1e-05
rotary_base = 10000.0

SEQ = ("q", "c")


def mm(a, b, ca, cb):
    return lax.dot_general(a, b, (((ca,), (cb,)), ((), ())), preferred_element_type=F32)


def swap(value, axis, count, k):
    return lax.ppermute(value, axis, [(i, i ^ k) for i in range(count)])


def after(value, *others):
    return lax.optimization_barrier((value, *others))[0]


def vmem_params(count):
    return pltpu.CompilerParams(
        dimension_semantics=("arbitrary",) * count, vmem_limit_bytes=60 * 1024 * 1024
    )


def held(shape, index_map):
    return pl.BlockSpec(shape, index_map, pipeline_mode=pl.Buffered(1))


def cost(flops, nbytes):
    return pl.CostEstimate(flops=int(flops), bytes_accessed=int(nbytes), transcendentals=0)


def pack_kernel(where, gate_ref, up_ref, *out_refs):
    planes = len(out_refs)
    size = gate_ref.shape[2] // planes
    for k in range(planes):
        columns = pl.ds(pl.multiple_of((where[0] ^ k) * size, 128), size)
        out_refs[k][:, :size] = gate_ref[0, :, columns]
        out_refs[k][:, size:] = up_ref[0, :, columns]


def pack_experts(where, w_gate, w_up, planes):
    experts, slab, full = w_gate.shape
    size = full // planes
    spec = pl.BlockSpec((1, slab, full), lambda e, s: (e, 0, 0))
    out = pl.BlockSpec((slab, 2 * size), lambda e, s: (0, e))
    return pl.pallas_call(
        pack_kernel,
        grid_spec=pltpu.PrefetchScalarGridSpec(
            num_scalar_prefetch=1, grid=(experts,), in_specs=[spec, spec], out_specs=[out] * planes
        ),
        out_shape=[jax.ShapeDtypeStruct((slab, 2 * experts * size), BF16)] * planes,
        compiler_params=vmem_params(1),
        name="pack",
    )(where, w_gate, w_up)


def place_kernel(where, *refs):
    out_ref = refs[-1]
    for k, piece in enumerate(refs[:-1]):
        size = piece.shape[0]
        out_ref[pl.ds(pl.multiple_of((where[0] ^ k) * size, 128), size), :] = piece[...]


def place_rows(where, pieces):
    rows, columns = pieces[0].shape
    full = rows * len(pieces)
    half = columns // 2
    return pl.pallas_call(
        place_kernel,
        grid_spec=pltpu.PrefetchScalarGridSpec(
            num_scalar_prefetch=1,
            grid=(2,),
            in_specs=[pl.BlockSpec((rows, half), lambda i, s: (0, i))] * len(pieces),
            out_specs=pl.BlockSpec((full, half), lambda i, s: (0, i)),
        ),
        out_shape=jax.ShapeDtypeStruct((full, columns), BF16),
        compiler_params=vmem_params(1),
        name="place",
    )(where, *pieces)


def unpack_kernel(where, *refs):
    gate_ref, up_ref = refs[-2:]
    size = refs[0].shape[1] // 2
    for k, piece in enumerate(refs[:-2]):
        columns = pl.ds(pl.multiple_of((where[0] ^ k) * size, 128), size)
        gate_ref[0, :, columns] = piece[:, :size].astype(F32)
        up_ref[0, :, columns] = piece[:, size:].astype(F32)


def unpack_experts(where, pieces, experts):
    slab, columns = pieces[0].shape
    size = columns // (2 * experts)
    full = size * len(pieces)
    spec = pl.BlockSpec((slab, 2 * size), lambda e, s: (0, e))
    out = pl.BlockSpec((1, slab, full), lambda e, s: (e, 0, 0))
    shape = jax.ShapeDtypeStruct((experts, slab, full), F32)
    return pl.pallas_call(
        unpack_kernel,
        grid_spec=pltpu.PrefetchScalarGridSpec(
            num_scalar_prefetch=1,
            grid=(experts,),
            in_specs=[spec] * len(pieces),
            out_specs=[out, out],
        ),
        out_shape=[shape, shape],
        compiler_params=vmem_params(1),
        name="unpack",
    )(where, *pieces)


def moe_kernel(count, experts, own_experts, aliased, where, *refs):
    x_refs, y_refs = refs[:count], refs[count : 2 * count]
    router_ref = refs[2 * count]
    gu_refs, down_refs = refs[2 * count + 1 : 2 * count + 3], refs[2 * count + 3 : 2 * count + 5]
    refs = refs[2 * count + 5 + (count if aliased else 0) :]
    dx_refs, out_refs = refs[:count], refs[count : 2 * count]
    act_out, grad_out = refs[2 * count : 2 * count + 2]
    xs, ys, gu_all, down_all, prob_sum, act_ref, grad_ref, sems, out_sems = refs[2 * count + 2 :]
    rows, width = x_refs[0].shape
    steps, size = down_all.shape[:2]

    for e in range(steps):
        side, i = divmod(e, own_experts)
        cols = slice(i * 2 * size, (i + 1) * 2 * size)
        lines = slice(i * size, (i + 1) * size)
        pltpu.make_async_copy(gu_refs[side].at[:, cols], gu_all.at[e], sems.at[0, e]).start()
        pltpu.make_async_copy(down_refs[side].at[lines, :], down_all.at[e], sems.at[1, e]).start()
    for i in range(count):
        here = slice(i * rows, (i + 1) * rows)
        xs[here, :] = x_refs[i][...]
        ys[here, :] = y_refs[i][:, :width]
    logits = mm(xs[...], router_ref[...], 1, 0)
    lane = lax.broadcasted_iota(jnp.int32, logits.shape, 1)
    logits = jnp.where(lane < experts, logits, -jnp.inf)
    spread = jnp.exp(logits - jnp.max(logits, axis=1, keepdims=True))
    probs = spread / jnp.sum(spread, axis=1, keepdims=True)
    weight = probs * jnp.concatenate([y[:, width:].astype(F32) for y in y_refs], axis=0)
    prob_sum[...] = jnp.zeros_like(prob_sum)

    def one_expert(e, carry):
        pltpu.make_async_copy(gu_all.at[e], gu_all.at[e], sems.at[0, e]).wait()
        pltpu.make_async_copy(down_all.at[e], down_all.at[e], sems.at[1, e]).wait()
        which = jnp.where(
            e < own_experts,
            where[1] * own_experts + e,
            (where[1] ^ 1) * own_experts + e - own_experts,
        )
        prob = jnp.sum(jnp.where(lane == which, weight, 0.0), axis=1, keepdims=True)
        both = mm(xs[...], gu_all[e], 1, 0)
        gate, up = both[:, :size], both[:, size:]
        sig = 1.0 / (1.0 + jnp.exp(-gate))
        back = mm(ys[...], down_all[e], 1, 1)
        silu = gate * sig
        act = silu * up
        prob_sum[...] += jnp.where(lane == which, jnp.sum(act * back, axis=1, keepdims=True), 0.0)
        back = back * prob
        act_ref[:, pl.ds(pl.multiple_of(e * size, size), size)] = (act * prob).astype(BF16)
        grad_ref[:, pl.ds(pl.multiple_of(2 * e * size, size), size)] = (
            back * up * sig * (1.0 + gate * (1.0 - sig))
        ).astype(BF16)
        grad_ref[:, pl.ds(pl.multiple_of((2 * e + 1) * size, size), size)] = (back * silu).astype(
            BF16
        )
        return carry

    lax.fori_loop(0, steps, one_expert, 0)
    leaving = [
        pltpu.make_async_copy(act_ref, act_out, out_sems.at[0]),
        pltpu.make_async_copy(grad_ref, grad_out, out_sems.at[1]),
    ]
    for copy in leaving:
        copy.start()
    tile = min(512, width)

    def one_tile(n, carry):
        cols = pl.ds(pl.multiple_of(n * tile, tile), tile)
        dx = out = None
        for e in range(steps):
            term = mm(grad_ref[:, 2 * e * size : 2 * (e + 1) * size], gu_all[e, cols, :], 1, 1)
            dx = term if dx is None else dx + term
            term = mm(act_ref[:, e * size : (e + 1) * size], down_all[e, :, cols], 1, 0)
            out = term if out is None else out + term
        for i in range(count):
            here = slice(i * rows, (i + 1) * rows)
            dx_refs[i][:, cols] = dx[here].astype(BF16)
            out_refs[i][:, cols] = out[here].astype(BF16)
        return carry

    lax.fori_loop(0, width // tile, one_tile, 0)
    for i in range(count):
        dx_refs[i][:, width:] = prob_sum[i * rows : (i + 1) * rows].astype(BF16)
    for copy in leaving:
        copy.wait()


def moe_rows(where, group, groups, xs, ys, router, gus, downs, outs, experts, own_experts):
    count = len(xs)
    rows, width = xs[0].shape
    size = downs[0].shape[0] // own_experts
    total = count * rows
    steps = 2 * own_experts
    lanes = router.shape[1]
    aliased = outs is not None

    def fixed(block):
        return lambda i, s: (block, 0)

    anywhere = pl.BlockSpec(memory_space=pl.ANY)
    in_specs = (
        [held((rows, width), fixed(0)) for _ in xs]
        + [held((rows, y.shape[1]), fixed(i)) for y, i in ys]
        + [held(router.shape, fixed(0))]
        + [anywhere] * 4
        + ([anywhere] * count if aliased else [])
    )
    out_specs = (
        [held((rows, width + lanes), fixed(0))] * count
        + [held((rows, width), fixed(group))] * count
        + [anywhere] * 2
    )
    first = 1 + 2 * count + 5
    return pl.pallas_call(
        functools.partial(moe_kernel, count, experts, own_experts, aliased),
        grid_spec=pltpu.PrefetchScalarGridSpec(
            num_scalar_prefetch=1,
            grid=(1,),
            in_specs=in_specs,
            out_specs=out_specs,
            scratch_shapes=[
                pltpu.VMEM((total, width), BF16),
                pltpu.VMEM((total, width), BF16),
                pltpu.VMEM((steps, width, 2 * size), BF16),
                pltpu.VMEM((steps, size, width), BF16),
                pltpu.VMEM((total, lanes), F32),
                pltpu.VMEM((total, steps * size), BF16),
                pltpu.VMEM((total, 2 * steps * size), BF16),
                pltpu.SemaphoreType.DMA((2, steps)),
                pltpu.SemaphoreType.DMA((2,)),
            ],
        ),
        out_shape=[jax.ShapeDtypeStruct((rows, width + lanes), BF16)] * count
        + [jax.ShapeDtypeStruct((groups * rows, width), BF16)] * count
        + [
            jax.ShapeDtypeStruct((total, steps * size), BF16),
            jax.ShapeDtypeStruct((total, 2 * steps * size), BF16),
        ],
        input_output_aliases={first + i: count + i for i in range(count)} if aliased else {},
        compiler_params=vmem_params(1),
        cost_estimate=cost(
            12 * total * width * size * steps, 8 * total * width + 6 * width * size * steps
        ),
        name="moe",
    )(where, *xs, *[y for y, _ in ys], router, *gus, *downs, *(outs or []))


def norm_ffn_kernel(token_ref, own_ref, *refs):
    gain_ref, res_ref, low_ref = refs[-3:]
    total = token_ref[...].astype(F32) + own_ref[...]
    for ref in refs[:-3]:
        total = total + ref[...].astype(F32)
    res_ref[...] = total
    scale = lax.rsqrt(jnp.mean(total * total, axis=1, keepdims=True) + epsilon)
    low_ref[...] = (total * scale * gain_ref[...]).astype(BF16)


def norm_ffn(tokens, own, parts, gain):
    return pl.pallas_call(
        norm_ffn_kernel,
        out_shape=[
            jax.ShapeDtypeStruct(tokens.shape, F32),
            jax.ShapeDtypeStruct(tokens.shape, BF16),
        ],
        compiler_params=vmem_params(0),
        cost_estimate=cost(10 * tokens.size, 16 * tokens.size),
        name="nffn",
    )(tokens, own, *parts, gain)


def norm_back_kernel(experts, low_ref, res_ref, router_ref, wide_ref, gain_ref, *refs):
    grad_ref, grad_low_ref, logit_ref, gain_out = refs[-4:]
    width = res_ref.shape[1]
    total = refs[0][...].astype(F32)
    for ref in refs[1:-4]:
        total = total + ref[...].astype(F32)
    upstream = wide_ref[:, :width].astype(F32)
    mask = wide_ref[:, width:].astype(F32)
    logits = mm(low_ref[...], router_ref[...], 1, 0)
    lane = lax.broadcasted_iota(jnp.int32, logits.shape, 1)
    logits = jnp.where(lane < experts, logits, -jnp.inf)
    spread = jnp.exp(logits - jnp.max(logits, axis=1, keepdims=True))
    probs = spread / jnp.sum(spread, axis=1, keepdims=True)
    prob_full = total[:, width:] * mask
    logit = (
        probs * (prob_full - jnp.sum(probs * prob_full, axis=1, keepdims=True))
    ).astype(BF16)
    logit_ref[...] = logit
    dn = total[:, :width] + mm(logit, router_ref[...], 1, 1)
    residual = res_ref[...]
    scale = lax.rsqrt(jnp.mean(residual * residual, axis=1, keepdims=True) + epsilon)
    scaled = dn * gain_ref[...]
    grad = upstream + (
        scaled * scale - residual * (scale**3 * jnp.mean(residual * scaled, axis=1, keepdims=True))
    )
    grad_ref[...] = grad
    grad_low_ref[...] = grad.astype(BF16)
    gain_out[...] = jnp.sum(dn * residual * scale, axis=0, keepdims=True)


def norm_back(low, residual, router, wide, gain, parts, experts):
    count, width = residual.shape
    return pl.pallas_call(
        functools.partial(norm_back_kernel, experts),
        out_shape=[
            jax.ShapeDtypeStruct((count, width), F32),
            jax.ShapeDtypeStruct((count, width), BF16),
            jax.ShapeDtypeStruct((count, router.shape[1]), BF16),
            jax.ShapeDtypeStruct((1, width), F32),
        ],
        compiler_params=vmem_params(0),
        cost_estimate=cost(20 * low.size, 30 * low.size),
        name="nback",
    )(low, residual, router, wide, gain, *parts)


def merge_kernel(planes, where, own_ref, other_ref, *out_refs):
    total = own_ref[...].astype(F32) + other_ref[...].astype(F32)
    k = pl.program_id(0)
    for i in range(planes):

        @pl.when(k == i)
        def _(i=i):
            out_refs[i][...] = total.astype(BF16)


def merge_parts(where, own, other, planes):
    slab, columns = own.shape[0] // planes, own.shape[1]
    spec = pl.BlockSpec((slab, columns), lambda k, s: (s[0] ^ k, 0))
    return pl.pallas_call(
        functools.partial(merge_kernel, planes),
        grid_spec=pltpu.PrefetchScalarGridSpec(
            num_scalar_prefetch=1,
            grid=(planes,),
            in_specs=[spec, spec],
            out_specs=[pl.BlockSpec((slab, columns), lambda k, s: (0, 0))] * planes,
        ),
        out_shape=[jax.ShapeDtypeStruct((slab, columns), BF16)] * planes,
        compiler_params=vmem_params(1),
        cost_estimate=cost(own.size, 6 * own.size),
        name="merge",
    )(where, own, other)


def grad_in_kernel(groups, count, where, *refs):
    x_refs = refs[: groups * count]
    g_refs = refs[groups * count : groups * count + groups]
    own_ref, other_ref, xs = refs[groups * count + groups :]
    rows = x_refs[0].shape[0]
    half = own_ref.shape[1]
    for i, x in enumerate(x_refs):
        xs[i * rows : (i + 1) * rows, :] = x[...]
    step = count * rows
    for out, start in ((own_ref, 0), (other_ref, half)):
        total = None
        for g in range(groups):
            term = mm(
                xs[g * step : (g + 1) * step, :], g_refs[g][:, start : start + half], 0, 0
            )
            total = term if total is None else total + term
        out[...] = total.astype(BF16)


def grad_in(where, xs, grads, tile=256):
    groups, count = len(grads), len(xs) // len(grads)
    rows, width = xs[0].shape
    columns = grads[0].shape[1]
    shape = jax.ShapeDtypeStruct((width, columns // 2), BF16)
    return pl.pallas_call(
        functools.partial(grad_in_kernel, groups, count),
        grid_spec=pltpu.PrefetchScalarGridSpec(
            num_scalar_prefetch=1,
            grid=(width // tile,),
            in_specs=[pl.BlockSpec((rows, tile), lambda i, s: (0, i))] * len(xs)
            + [held(g.shape, lambda i, s: (0, 0)) for g in grads],
            out_specs=[pl.BlockSpec((tile, columns // 2), lambda i, s: (i, 0))] * 2,
            scratch_shapes=[pltpu.VMEM((rows * len(xs), tile), BF16)],
        ),
        out_shape=[shape, shape],
        compiler_params=vmem_params(1),
        cost_estimate=cost(
            2 * rows * len(xs) * width * columns, 2 * rows * len(xs) * (width + columns)
        ),
        name="gin",
    )(where, *xs, *grads)


def grad_down_kernel(places, own_steps, where, *refs):
    y_refs = refs[: len(places)]
    groups = len(refs) - len(places) - 3
    a_refs = refs[len(places) : len(places) + groups]
    own_ref, other_ref, ys = refs[len(places) + groups :]
    e = pl.program_id(1)

    @pl.when(e == 0)
    def _():
        for ref, there in zip(y_refs, places):
            size = ref.shape[0] // len(there)
            for i, place in enumerate(there):
                ys[place * size : (place + 1) * size, :] = ref[i * size : (i + 1) * size, :]

    step = a_refs[0].shape[0]
    total = None
    for g in range(groups):
        term = mm(a_refs[g][...], ys[g * step : (g + 1) * step, :], 0, 0)
        total = term if total is None else total + term

    @pl.when(e < own_steps)
    def _():
        own_ref[...] = total

    @pl.when(e >= own_steps)
    def _():
        other_ref[...] = total.astype(BF16)


def grad_down_rows(where, ys, places, acts, width, own_experts):
    size = acts[0].shape[1] // (2 * own_experts)
    last = own_experts - 1
    total = acts[0].shape[0] * len(acts)
    tile = width
    while total * tile > 1 << 21:
        tile //= 2
    return pl.pallas_call(
        functools.partial(grad_down_kernel, places, own_experts),
        grid_spec=pltpu.PrefetchScalarGridSpec(
            num_scalar_prefetch=1,
            grid=(width // tile, 2 * own_experts),
            in_specs=[pl.BlockSpec((y.shape[0], tile), lambda j, e, s: (0, j)) for y in ys]
            + [pl.BlockSpec((a.shape[0], size), lambda j, e, s: (0, e)) for a in acts],
            out_specs=[
                pl.BlockSpec((size, tile), lambda j, e, s: (jnp.minimum(e, last), j)),
                pl.BlockSpec((size, tile), lambda j, e, s: (jnp.maximum(e - own_experts, 0), j)),
            ],
            scratch_shapes=[pltpu.VMEM((total, tile), BF16)],
        ),
        out_shape=[
            jax.ShapeDtypeStruct((own_experts * size, width), F32),
            jax.ShapeDtypeStruct((own_experts * size, width), BF16),
        ],
        compiler_params=vmem_params(2),
        cost_estimate=cost(
            4 * total * width * size * own_experts, 2 * total * (width + 2 * size * own_experts)
        ),
        name="gdown",
    )(where, *ys, *acts)


def block_rows(seq, block, seqs, size):
    k = seq ^ block
    return pl.ds(pl.multiple_of(((k & 1) * (seqs // 2) + (k >> 1)) * size, size), size)


def turned(values, cosine, sine):
    return values * cosine + pltpu.roll(values, values.shape[1] // 2, 1) * sine


def attend_kernel(seqs, tile, where, q_ref, k_ref, v_ref, scale_ref, gain_ref, cos_ref, sin_ref, att_ref, ql, kl, vl, lse_ref):
    length, head = q_ref.shape
    size = length // seqs
    for b in range(seqs):
        rows = block_rows(where[1], b, seqs, size)
        here = slice(b * size, (b + 1) * size)
        cosine, sine = cos_ref[here, :], sin_ref[here, :]
        scales = scale_ref[here, :]
        ql[here, :] = turned(
            q_ref[rows, :] * scales[:, 0:1] * gain_ref[0:1, :], cosine, sine
        ).astype(BF16)
        kl[here, :] = turned(
            k_ref[rows, :] * scales[:, 1:2] * gain_ref[1:2, :], cosine, sine
        ).astype(BF16)
        vl[here, :] = v_ref[rows, :].astype(BF16)
    diagonal = lax.broadcasted_iota(jnp.int32, (tile, tile), 0) >= lax.broadcasted_iota(
        jnp.int32, (tile, tile), 1
    )
    for t in range(length // tile):
        here = slice(t * tile, (t + 1) * tile)
        limit = (t + 1) * tile
        scores = mm(ql[here, :], kl[:limit, :], 1, 1) * (head ** (-0.5))
        edge = jnp.where(diagonal, scores[:, t * tile :], -jnp.inf)
        scores = jnp.concatenate([scores[:, : t * tile], edge], axis=1) if t else edge
        peak = jnp.max(scores, axis=1, keepdims=True)
        spread = jnp.exp(scores - peak)
        total = jnp.sum(spread, axis=1, keepdims=True)
        weights = (spread * (1.0 / total)).astype(BF16)
        out = mm(weights, vl[:limit, :], 1, 0).astype(BF16)
        lse_ref[here, :] = jnp.broadcast_to(peak + jnp.log(total), (tile, head))
        for b in range(tile // size):
            rows = block_rows(where[1], t * (tile // size) + b, seqs, size)
            att_ref[rows, :] = out[b * size : (b + 1) * size]


def attend(where, projected, scales, gain_rows, cosine, sine, seqs, heads, tile=256):
    length = projected.shape[0]
    head = projected.shape[1] // (3 * heads)
    part = heads * head

    def column(offset):
        return pl.BlockSpec((length, head), lambda h, s: (0, offset + h))

    full = pl.BlockSpec((length, head), lambda h, s: (0, 0))
    low = jax.ShapeDtypeStruct((length, part), BF16)
    return pl.pallas_call(
        functools.partial(attend_kernel, seqs, tile),
        grid_spec=pltpu.PrefetchScalarGridSpec(
            num_scalar_prefetch=1,
            grid=(heads,),
            in_specs=[
                column(0),
                column(heads),
                column(2 * heads),
                pl.BlockSpec(scales.shape, lambda h, s: (0, 0)),
                pl.BlockSpec((2, head), lambda h, s: (0, h)),
                full,
                full,
            ],
            out_specs=[column(0)] * 5,
        ),
        out_shape=[low, low, low, low, jax.ShapeDtypeStruct((length, part), F32)],
        compiler_params=vmem_params(1),
        cost_estimate=cost(4 * length * length * part, 20 * length * part),
        name="att",
    )(where, projected, projected, projected, scales, gain_rows, cosine, sine)


def attend_back_kernel(seqs, tile, where, q_ref, k_ref, v_ref, lse_ref, grad_ref, cos_ref, sin_ref, dq_ref, dk_ref, dv_ref, go, dk, dv):
    length, head = q_ref.shape
    size = length // seqs
    scale = head ** (-0.5)
    for b in range(seqs):
        go[b * size : (b + 1) * size, :] = grad_ref[block_rows(where[1], b, seqs, size), :]
    dk[...] = jnp.zeros_like(dk)
    dv[...] = jnp.zeros_like(dv)
    diagonal = lax.broadcasted_iota(jnp.int32, (tile, tile), 0) >= lax.broadcasted_iota(
        jnp.int32, (tile, tile), 1
    )
    for t in range(length // tile):
        here = slice(t * tile, (t + 1) * tile)
        limit = (t + 1) * tile
        scores = mm(q_ref[here, :], k_ref[:limit, :], 1, 1) * scale
        edge = jnp.where(diagonal, scores[:, t * tile :], -jnp.inf)
        scores = jnp.concatenate([scores[:, : t * tile], edge], axis=1) if t else edge
        probs = jnp.exp(scores - lse_ref[here, 0:1])
        dprobs = mm(go[here, :], v_ref[:limit, :], 1, 1)
        terms = probs * dprobs
        dscores = (terms - probs * jnp.sum(terms, axis=1, keepdims=True)).astype(BF16)
        dq = (mm(dscores, k_ref[:limit, :], 1, 0) * scale).astype(BF16).astype(F32)
        dq = turned(dq, cos_ref[here, :], -sin_ref[here, :])
        for b in range(tile // size):
            rows = block_rows(where[1], t * (tile // size) + b, seqs, size)
            dq_ref[rows, :] = dq[b * size : (b + 1) * size]
        dk[:limit, :] += mm(dscores, q_ref[here, :], 0, 0)
        dv[:limit, :] += mm(probs.astype(BF16), go[here, :], 0, 0)
    for b in range(seqs):
        here = slice(b * size, (b + 1) * size)
        rows = block_rows(where[1], b, seqs, size)
        back = (dk[here, :] * scale).astype(BF16).astype(F32)
        dk_ref[rows, :] = turned(back, cos_ref[here, :], -sin_ref[here, :])
        dv_ref[rows, :] = dv[here, :].astype(BF16)


def attend_back(where, ql, kl, vl, lse, grads, cosine, sine, seqs, heads, tile=256):
    length, part = ql.shape
    head = part // heads
    column = pl.BlockSpec((length, head), lambda h, s: (0, h))
    full = pl.BlockSpec((length, head), lambda h, s: (0, 0))
    wide = jax.ShapeDtypeStruct((length, part), F32)
    return pl.pallas_call(
        functools.partial(attend_back_kernel, seqs, tile),
        grid_spec=pltpu.PrefetchScalarGridSpec(
            num_scalar_prefetch=1,
            grid=(heads,),
            in_specs=[column] * 5 + [full, full],
            out_specs=[column] * 3,
            scratch_shapes=[
                pltpu.VMEM((length, head), BF16),
                pltpu.VMEM((length, head), F32),
                pltpu.VMEM((length, head), F32),
            ],
        ),
        out_shape=[wide, wide, jax.ShapeDtypeStruct((length, part), BF16)],
        compiler_params=vmem_params(1),
        cost_estimate=cost(10 * length * length * part, 24 * length * part),
        name="aback",
    )(where, ql, kl, vl, lse, grads, cosine, sine)


def seq_gather(block, chips):
    near = [block] + [swap(block, "q", chips, k) for k in range(1, chips)]
    near = jnp.concatenate(near, axis=0)
    return near, swap(near, "c", 2, 1)


def seq_parts(own, other, chips):
    total = own + swap(other, "c", 2, 1).astype(F32)
    rows = total.shape[0] // chips
    low = total[rows:].astype(BF16)
    parts = [swap(low[(k - 1) * rows : k * rows], "q", chips, k) for k in range(1, chips)]
    return total[:rows], parts


def masks_of(planes):
    return [3, 1] if planes == 4 else [1 << i for i in range(planes.bit_length() - 1)]


def plane_gather(block, planes):
    rows = block.shape[0]
    have, parts = {0: (block, 0)}, [(block, [0])]
    for mask in masks_of(planes):
        keys = [k for _, ks in parts for k in ks]
        sent = parts[0][0] if len(parts) == 1 else jnp.concatenate([a for a, _ in parts], axis=0)
        arrived = swap(sent, "f", planes, mask)
        keys = [k ^ mask for k in keys]
        parts.append((arrived, keys))
        have.update({k: (arrived, j) for j, k in enumerate(keys)})
    return have, parts[1:], rows


def plane_reduce(blocks, planes):
    held_back = dict(enumerate(blocks))
    for i, mask in enumerate(reversed(masks_of(planes))):
        span = {0}
        for other in masks_of(planes)[: len(masks_of(planes)) - 1 - i]:
            span |= {k ^ other for k in span}
        keys = sorted(span)
        sent = jnp.concatenate([held_back[k ^ mask].astype(BF16) for k in keys], axis=0)
        rows = sent.shape[0] // len(keys)
        arrived = swap(sent, "f", planes, mask)
        held_back = {
            k: held_back[k] + arrived[j * rows : (j + 1) * rows].astype(F32)
            for j, k in enumerate(keys)
        }
    return held_back[0]


def by_bits(values, index, axis):
    size = values.shape[axis]
    bit = 1
    while bit < size:
        pieces = [lax.slice_in_dim(values, i, i + bit, axis=axis) for i in range(0, size, bit)]
        turned_over = jnp.concatenate([pieces[i ^ 1] for i in range(len(pieces))], axis=axis)
        values = jnp.where((index & bit) > 0, turned_over, values)
        bit *= 2
    return values


def to_position(values, seq, chips):
    n = values.shape[0]
    values = values.reshape(n, 2, chips, -1)
    values = by_bits(by_bits(values, seq & 1, 1), seq >> 1, 2)
    return values.swapaxes(1, 2).reshape(n, -1)


def from_position(values, seq, chips):
    n = values.shape[0]
    values = values.reshape(n, chips, 2, -1).swapaxes(1, 2)
    return by_bits(by_bits(values, seq & 1, 1), seq >> 1, 2).reshape(n, -1)


def small_sum(pair, seq, chips, rider=None):
    flat = to_position(pair, seq, chips).reshape(-1, LANES)
    count = flat.shape[0]
    if rider is not None:
        flat = jnp.concatenate([flat, rider.reshape(-1, LANES)], axis=0)
    every = lax.all_gather(flat, SEQ, axis=0)
    total = jnp.sum(every[:, :count], axis=0).reshape(pair.shape)
    return total if rider is None else (total, every[:, count:])


def shards(tokens, cotangent, gains, w_qkv, w_out, w_router, w_gate, w_up, w_down, routes):
    planes = lax.axis_size("f")
    chips = lax.axis_size("q")
    seqs = 2 * chips
    plane = lax.axis_index("f")
    seq = 2 * lax.axis_index("q") + lax.axis_index("c")
    where = jnp.stack([plane, seq]).astype(jnp.int32)
    count, width = tokens.shape
    length = count * seqs
    part = width // seqs
    heads = part // HEAD
    rows = w_qkv.shape[0]
    expert_count = w_router.shape[1]
    own_experts, _ = w_gate.shape[:2]
    slice_ff = w_down.shape[1]
    cut = own_experts * slice_ff

    columns = w_qkv.reshape(rows, 3, seqs, part).transpose(2, 0, 1, 3).reshape(seqs, rows, 3 * part)
    router_wide = jnp.pad(w_router, ((0, 0), (0, LANES - expert_count)))
    columns = jnp.concatenate(
        [columns, jnp.broadcast_to(router_wide, (seqs, rows, LANES))], axis=2
    )
    columns = lax.all_to_all(columns, SEQ, split_axis=0, concat_axis=0, tiled=True)

    mask = jnp.sum(
        (routes[:, :, None] == jnp.arange(expert_count, dtype=jnp.int32)[None, None, :]).astype(F32),
        axis=1,
    )
    wide = jnp.concatenate(
        [cotangent, jnp.pad(mask, ((0, 0), (0, LANES - expert_count))).astype(BF16)], axis=1
    )
    _, dy_parts, _ = plane_gather(wide, planes)

    inputs = tokens.astype(F32)
    in_scale = lax.rsqrt(jnp.mean(inputs * inputs, axis=-1, keepdims=True) + epsilon)
    normed_own = (inputs * in_scale * gains[0]).astype(BF16)
    near, far = seq_gather(after(normed_own, columns), chips)
    normed_attn = jnp.concatenate([near, far], axis=0)
    dy_far = []
    for value, there in dy_parts:
        dy_far.append(([value] + [swap(value, "q", chips, k) for k in range(1, chips)], there))
    dy_near = [wide] + [swap(wide, "q", chips, k) for k in range(1, chips)]

    columns = columns.reshape(seqs * rows, 3 * part + LANES)
    router_own = columns[:, 3 * part :]
    columns = after(columns[:, : 3 * part], dy_parts[-1][0])
    qkv_part = lax.all_gather(columns, "f", axis=0, tiled=True)
    nearest = sorted(range(1, planes), key=lambda k: -k if planes == 4 and k == 3 else k)
    out_z, router = {0: w_out}, {0: router_own}
    for k in nearest:
        out_z[k] = swap(w_out, "f", planes, k)
    for k in nearest:
        router[k] = swap(router_own, "f", planes, k)
    out_z = jnp.stack([out_z[k] for k in range(planes)])
    router = jnp.stack([router[k] for k in range(planes)])
    router = by_bits(router, plane, 0).reshape(width, LANES)

    half = seqs // 2
    lanes = seqs // planes
    b_of = seq % half
    here_f = seq // lanes
    blocks = []
    for j in range(planes):
        pairs = [
            (half * s + (f - j) % planes, lanes * f + s) for f in range(planes) for s in range(lanes)
        ]
        block = lax.dynamic_index_in_dim(
            out_z, ((b_of + j) % planes) ^ plane, 0, keepdims=False
        )
        blocks.append(lax.ppermute(block, SEQ, pairs))
    order = (here_f - jnp.arange(planes)) % planes
    out_rows = jnp.take(jnp.stack(blocks), order, axis=0).reshape(part, width)

    packed = pack_experts(where, w_gate, w_up, planes)
    qkv_part, *packed = lax.optimization_barrier((qkv_part, *packed))
    arrived = [packed[0]]
    for k in range(1, planes):
        arrived.append(swap(packed[k], "f", planes, k))
    own_gu = place_rows(where, arrived)
    other_gu = swap(own_gu, "c", 2, 1)
    own_down = w_down.reshape(cut, width)
    other_down = swap(own_down, "c", 2, 1)

    exponent_index = jnp.arange(HEAD // 2, dtype=F32) * (2.0 / HEAD)
    angles = jnp.arange(length, dtype=F32)[:, None] * (rotary_base ** (-exponent_index))[None, :]
    cosine, sine = jnp.cos(angles), jnp.sin(angles)
    cosine = jnp.concatenate([cosine, cosine], axis=1)
    sine = jnp.concatenate([-sine, sine], axis=1)
    cosine, sine = lax.optimization_barrier((cosine, sine))

    projected = mm(normed_attn, qkv_part, 1, 0)
    queries, keys = projected[:, :part], projected[:, part : 2 * part]
    squares = jnp.stack([jnp.sum(queries * queries, axis=1), jnp.sum(keys * keys, axis=1)])
    scales = lax.rsqrt(small_sum(squares, seq, chips) / width + epsilon)
    gain_rows = lax.dynamic_slice_in_dim(gains[1:3], seq * part, part, axis=1)
    attended, ql, kl, vl, lse = attend(
        where, projected, scales.T, gain_rows, cosine, sine, seqs, heads
    )
    group = chips * count
    out_other = mm(attended[group:], out_rows, 1, 0).astype(BF16)
    out_own = mm(attended[:group], out_rows, 1, 0)
    own, parts = seq_parts(out_own, out_other, chips)
    gain_ffn = gains[3:4]
    residual, normed_low = norm_ffn(tokens, own, parts, gain_ffn)

    x_blocks, x_planes = [], {}
    for f in range(planes):
        block = normed_low
        if planes == 4 and f == 2:
            block = swap(x_planes[3], "f", planes, 1)
        elif f:
            block = x_planes[f] if f in x_planes else swap(normed_low, "f", planes, f)
        if planes == 4 and f == 1:
            x_planes[3] = swap(normed_low, "f", planes, 3)
        x_blocks.append([block] + [swap(block, "q", chips, k) for k in range(1, chips)])

    acts, grads, outs, back_parts = [], [], None, []
    tight = planes * chips > 16
    for f in range(planes):
        if tight and f > 1:
            x_blocks[f][0] = after(x_blocks[f][0], back_parts[-1])
        if f == 0:
            ys = [(y, 0) for y in dy_near]
        else:
            ys = [(y, there.index(f)) for some, there in dy_far if f in there for y in some]
        results = moe_rows(
            where,
            f,
            planes,
            x_blocks[f],
            ys,
            router,
            [own_gu, other_gu],
            [own_down, other_down],
            outs,
            expert_count,
            own_experts,
        )
        dxs, outs = results[:chips], results[chips : 2 * chips]
        acts.append(results[2 * chips])
        grads.append(results[2 * chips + 1])
        arrivals = [dxs[0]] + [swap(dxs[k], "q", chips, k) for k in range(1, chips)]
        if f:
            if planes == 4 and f == 3:
                arrivals.append(from_next)
            total = sum(a.astype(F32) for a in arrivals).astype(BF16)
            mask = 1 if planes == 4 and f == 2 else f
            arrivals = [swap(total, "f", planes, mask)]
            if planes == 4 and f == 2:
                from_next, arrivals = arrivals[0], []
        back_parts += arrivals

    groups = max(planes // 2, 1)
    block = groups * count
    total = residual
    for g in reversed(range(planes // groups)):
        pieces = []
        for k in reversed(range(1, chips)):
            pieces.append(swap(outs[k][g * block : (g + 1) * block], "q", chips, k))
        moe = after(outs[0][g * block : (g + 1) * block], *pieces).astype(F32)
        moe = moe + sum(piece.astype(F32) for piece in pieces)
        pieces = [moe[i * count : (i + 1) * count] for i in range(groups)]
        if planes == 4 and g:
            arrived = swap(pieces[0].astype(BF16), "f", planes, 1).astype(F32)
            total = total + swap((pieces[1] + arrived).astype(BF16), "f", planes, 3).astype(F32)
            continue
        for k, piece in enumerate(pieces, g * groups):
            if k:
                piece = swap(piece.astype(BF16), "f", planes, k).astype(F32)
            total = total + piece
    output = total.astype(BF16)

    x_flat = [block for group_blocks in x_blocks for block in group_blocks]
    own_part, other_part = grad_in(where, x_flat, grads)
    other_part = swap(other_part, "c", 2, 1)
    back = list(merge_parts(where, own_part, other_part, planes))
    for k in range(1, planes):
        back[k] = swap(back[k], "f", planes, k)
    grad_gate, grad_up = unpack_experts(where, back, own_experts)
    places = [[k] for k in range(chips)]
    dy_all = list(dy_near)
    for dy_some, there in dy_far:
        dy_all += dy_some
        places += [[f * chips + k for f in there] for k in range(chips)]
    down_own, down_other = grad_down_rows(where, dy_all, places, acts, width, own_experts)
    down_other = swap(down_other, "c", 2, 1)
    grad_down = (down_own + down_other.astype(F32)).reshape(own_experts, slice_ff, width)

    if tight:
        back_parts[0] = after(back_parts[0], output, down_other, *back)

    res_grad, res_low, logit_wide, gain3 = norm_back(
        normed_low, residual, router, wide, gain_ffn, back_parts, expert_count
    )

    res_near, res_far = seq_gather(res_low, chips)
    attended_grad = jnp.concatenate(
        [mm(res_near, out_rows, 1, 1), mm(res_far, out_rows, 1, 1)], axis=0
    ).astype(BF16)
    query_back, key_back, value_low = attend_back(
        where, ql, kl, vl, lse, attended_grad, cosine, sine, seqs, heads
    )
    query_gg, key_gg = query_back * gain_rows[0], key_back * gain_rows[1]
    dots = jnp.stack([jnp.sum(queries * query_gg, axis=1), jnp.sum(keys * key_gg, axis=1)])
    value_term = mm(normed_attn, value_low, 0, 0).astype(BF16)
    value_term, dots = lax.optimization_barrier((value_term, dots))
    value_term = lax.psum_scatter(value_term, "f", scatter_dimension=0, tiled=True)
    scales = from_position(scales, seq, chips).T
    query_scale, key_scale = scales[:, 0:1], scales[:, 1:2]
    gain1 = jnp.sum(query_back * queries * query_scale, axis=0)
    gain2 = jnp.sum(key_back * keys * key_scale, axis=0)
    dots, gain_qk = small_sum(dots, seq, chips, jnp.stack([gain1, gain2]))
    dots = from_position(dots / width, seq, chips).T
    query_pre = query_gg * query_scale - queries * (query_scale**3 * dots[:, 0:1])
    key_pre = key_gg * key_scale - keys * (key_scale**3 * dots[:, 1:2])
    pre_low = jnp.concatenate([query_pre.astype(BF16), key_pre.astype(BF16)], axis=1)
    qk_term = mm(normed_attn, pre_low, 0, 0).astype(BF16)
    qk_term = lax.psum_scatter(qk_term, "f", scatter_dimension=0, tiled=True)
    projected_grad = jnp.concatenate([pre_low, value_low], axis=1)
    back_other = mm(projected_grad[group:], qkv_part, 1, 1).astype(BF16)
    back_own = mm(projected_grad[:group], qkv_part, 1, 1)
    own, parts = seq_parts(back_own, back_other, chips)
    attn_back = own + sum(p.astype(F32) for p in parts)
    scaled = attn_back * gains[0]
    grad_tokens = res_grad + (
        scaled * in_scale - inputs * in_scale**3 * jnp.mean(inputs * scaled, axis=-1, keepdims=True)
    )

    attended_both = attended
    res_both = jnp.concatenate([res_near, res_far], axis=0)
    out_term = mm(attended_both, res_both, 0, 0).astype(BF16).reshape(planes, rows, width)
    pieces = []
    for j in range(planes):
        pairs = [
            (lanes * f + s, half * s + (f - j) % planes) for f in range(planes) for s in range(lanes)
        ]
        block = lax.dynamic_index_in_dim(out_term, (here_f - j) % planes, 0, keepdims=False)
        pieces.append(lax.ppermute(block, SEQ, pairs))
    pieces = jnp.stack(pieces)
    grad_out = plane_reduce(
        [
            lax.dynamic_index_in_dim(pieces, ((plane ^ k) - b_of) % planes, 0, keepdims=False).astype(F32)
            for k in range(planes)
        ],
        planes,
    )

    gain3 = gain3[0]
    gain_high = gain3.astype(BF16)
    gain_low = (gain3 - gain_high.astype(F32)).astype(BF16)
    extra = jnp.concatenate(
        [logit_wide, gain_high.reshape(-1, LANES), gain_low.reshape(-1, LANES)], axis=0
    )
    extras = [extra] + [swap(extra, "q", chips, k) for k in range(1, chips)]
    logit_near = jnp.concatenate([e[:count] for e in extras], axis=0)
    x_near = jnp.concatenate(x_blocks[0], axis=0)
    router_term = mm(x_near, logit_near, 0, 0)
    gain_term = sum(e[count:].astype(F32) for e in extras)
    gain_term = jnp.sum(gain_term.reshape(2, width), axis=0)
    small = jnp.concatenate(
        [router_term[:, :expert_count], gain_term[:, None]], axis=1
    ).reshape(planes, seqs, rows, expert_count + 1)
    small_own = lax.dynamic_index_in_dim(small, seq, 1, keepdims=False)
    small_other = lax.dynamic_index_in_dim(small, seq ^ 1, 1, keepdims=False)
    small_own = small_own + swap(small_other, "c", 2, 1)
    small_sum_z = lax.dynamic_index_in_dim(small_own, plane, 0, keepdims=False)
    for k in range(1, planes):
        piece = lax.dynamic_index_in_dim(small_own, plane ^ k, 0, keepdims=False)
        small_sum_z = small_sum_z + swap(piece, "f", planes, k)
    grad_router = small_sum_z[:, :expert_count]

    back_qkv = jnp.concatenate([qk_term, value_term], axis=1).reshape(seqs, rows, 3 * part)
    grad_qkv = lax.all_to_all(back_qkv, SEQ, split_axis=0, concat_axis=0, tiled=True)
    grad_qkv = (
        grad_qkv.reshape(seqs, rows, 3, part)
        .transpose(1, 2, 0, 3)
        .reshape(rows, 3 * width)
        .astype(F32)
    )
    gain_qk = gain_qk.reshape(seqs, 2, part).swapaxes(0, 1)
    gain_qk = lax.dynamic_index_in_dim(gain_qk.reshape(2, planes, seqs, rows), seq, 2, keepdims=False)
    gain_sum = lax.dynamic_index_in_dim(gain_qk, plane, 1, keepdims=False)
    for k in range(1, planes):
        piece = lax.dynamic_index_in_dim(gain_qk, plane ^ k, 1, keepdims=False)
        gain_sum = gain_sum + swap(piece, "f", planes, k)
    own_gain = lax.dynamic_slice_in_dim(gains[0], (plane * seqs + seq) * rows, rows)
    gain0 = jnp.sum(w_qkv.astype(F32) * grad_qkv, axis=1) / own_gain
    grad_gains = jnp.concatenate(
        [gain0[None], gain_sum, small_sum_z[:, expert_count][None]], axis=0
    )
    return (
        output,
        grad_tokens,
        grad_gains,
        grad_qkv,
        grad_out,
        grad_router,
        grad_gate,
        grad_up,
        grad_down,
    )


def solution(mesh):
    devices = mesh.devices
    inner = Mesh(devices.reshape(devices.shape[0], devices.shape[1] // 2, 2), ("f", "q", "c"))
    all_axes = ("f", "q", "c")
    by_rows = P(all_axes, None)
    expert = P(SEQ, "f", None)

    return jax.shard_map(
        shards,
        mesh=inner,
        in_specs=(by_rows, by_rows, P(), by_rows, by_rows, by_rows, expert, expert, expert, by_rows),
        out_specs=(
            by_rows,
            by_rows,
            P(None, all_axes),
            by_rows,
            by_rows,
            by_rows,
            expert,
            expert,
            expert,
        ),
        check_vma=False,
    )
```
